256 devices in a mesh: cells: 16 (over x, y), levels: 16 (over z, core).
Axes of the slice: x: 4, y: 4, z: 8, core: 2. Of those that a mesh axis runs over, the one named last changes fastest.
Arguments:
- populations: float32 [8192, 4096], P('cells', 'levels'), may hold values from 0.05 to 2
- face_speed: float32 [8193], replicated, may hold values from -1 to 1
- cell_class: int32 [8192, 1], P('cells'), may hold values from 0 to 15; in each aligned block of 512 rows (0 to 511, 512 to 1023, ...) at most 64 rows name the same one
- class_offset: bfloat16 [8192], P('cells'), may hold values from -1 to 1
- rate_matrix: bfloat16 [16, 4096, 4096], P('cells', 'levels'), may hold values from -0.09375 to 0.09375
- slope_matrix: bfloat16 [16, 4096, 4096], P('cells', 'levels'), may hold values from -0.09375 to 0.09375
- rate_scale: float32 [16, 4096], P('cells', 'levels'), may hold values from 0.2 to 2
- slope_scale: float32 [16, 4096], P('cells', 'levels'), may hold values from 0.2 to 2
Outputs:
- sources: float32 [8192, 4096], P('cells', 'levels')
- updated: float32 [8192, 4096], P('cells', 'levels')
The draws below stay inside these ranges and needn't reach their ends.
Inputs may be any that keep to these rules, and one draw needn't show every extreme that they name: `cell_class`: among the cells of one index of the cells axis (aligned blocks of 512 cells) no class is named by more than 64 cells.
All inputs are finite; a program needn't handle non-finite values.
Results may differ from the reference program's by a relative error of at most 0.0029.
Values may be sent and summed in bfloat16 or wider, within the bound.
A program may use at most 64 MiB of HBM per device.

```python
import math
import jax
import jax.numpy as jnp
import numpy as np
from jax import lax

CELL_DEV = 512
L = 4096
CELLS = 8192
CLASSES = 16
CAP = 64
N_CELLS = 16


def level_of(own_key, shape, split, least, top_value):
    def one(axis_at, blocks):
        heights = jax.random.uniform(jax.random.fold_in(jax.random.fold_in(own_key, 6), axis_at), (blocks,), jnp.float32, least / len(split), top_value / len(split))
        return jnp.repeat(jnp.exp(heights), shape[axis_at] // blocks).reshape((-1,) + (1,) * (len(shape) - axis_at - 1))

    level = one(*split[0])
    for cut in split[1:]:
        level = level * one(*cut)
    return level


def routed_block(stream_key, own, number, rows, count, top, bound, lean):
    sequence = jax.random.permutation(stream_key, count)
    packed, usual = portions_of(count, rows * top, bound, lean, True), portions_of(count, rows * top, bound, lean, False)
    places = jnp.arange(count)

    def named(tallies, rotation):
        used = int((tallies > 0).sum())
        fixed = max(1, used // 4)
        shifted = fixed + (places - fixed + rotation * (used - fixed)) % max(1, count - fixed)
        return jnp.zeros((count,), jnp.int32).at[sequence[jnp.where(places < fixed, places, shifted)]].set(jnp.asarray(tallies, jnp.int32))

    tallies = jnp.where(number % 4 == 0, named(packed, number // 4), named(usual, number - number // 4 - 1))
    mixed = jax.random.permutation(jax.random.fold_in(own, 3), count)
    donor, taker = mixed[0:count // 2 * 2:2], mixed[1:count // 2 * 2:2]
    margin = jnp.minimum(tallies[donor] - 1, bound - tallies[taker]) // 2
    margin = jnp.where((donor == sequence[0]) | (taker == sequence[0]) | (tallies[taker] == 0), 0, jnp.maximum(margin, 0))
    shifted = jax.random.randint(jax.random.fold_in(own, 4), (count // 2,), 0, 1 << 20) % (margin + 1)
    tallies = tallies.at[donor].add(-shifted).at[taker].add(shifted)
    members = jnp.searchsorted(jnp.cumsum(tallies), jnp.arange(rows * top), side="right").astype(jnp.int32)
    table = members.reshape(top, rows).T
    table = table[jax.random.permutation(jax.random.fold_in(own, 1), rows)]
    rotation = jax.random.randint(jax.random.fold_in(own, 2), (rows, 1), 0, top)
    return jnp.take_along_axis(table, (jnp.arange(top)[None, :] + rotation) % top, axis=1)


def portions_of(number_of, total, limit, skew, full):
    weights = [(1 << 20) // math.isqrt(standing ** skew) + 1 for standing in range(1, number_of + 1)]
    largest = limit if full else min(limit, max(-(-total // number_of), total * weights[0] // sum(weights)))
    least = 1 if total - largest >= number_of - 1 else 0
    holding, rest = [largest] + [least] * (number_of - 1), total - largest - least * (number_of - 1)
    while rest > 0:
        candidates = [i for i in range(1, number_of) if holding[i] < largest] or [i for i in range(1, number_of) if holding[i] < limit]
        whole, left = sum([weights[i] for i in candidates]), rest
        for i in candidates:
            addition = min(limit - holding[i], max(1, left * weights[i] // whole), rest)
            holding[i] = holding[i] + addition
            rest = rest - addition
    return np.array(holding)


def bell_draw(stream_key, extent, width, limit, split=(), kind=jnp.bfloat16):
    array = width * jax.random.normal(stream_key, extent, jnp.float32)
    if split:
        array = array * level_of(stream_key, extent, split, -0.22, 0.18)
    return jnp.clip(array, -limit, limit).astype(kind)


def setup_inputs(seed: int = 0) -> dict:
    keys = jax.random.split(jax.random.key(seed), 9)
    populations = jnp.clip(jnp.exp(math.log(2.0) - 3.6888794 * jax.random.uniform(keys[0], (CELLS, L), jnp.float32) ** level_of(keys[0], (CELLS, L), ((0, 16), (1, 16)), -0.2, 0.2)), 0.05, 2.0)
    face_speed = jnp.clip(jax.random.uniform(keys[1], (CELLS + 1,), jnp.float32, -1.0, 1.0), -1.0, 1.0)
    cell_class_keys = jax.random.split(jax.random.fold_in(keys[2], 1), CELLS // CELL_DEV)
    cell_class_turns = jax.random.permutation(jax.random.fold_in(keys[2], 3), CELLS // CELL_DEV)
    cell_class = jax.vmap(lambda own, number: routed_block(jax.random.fold_in(keys[2], 2), own, number, CELL_DEV, CLASSES, 1, CAP, 2))(cell_class_keys, cell_class_turns).reshape((CELLS, 1))
    class_offset = jnp.clip(jax.random.uniform(keys[3], (CELLS,), jnp.float32, -1.0, 1.0) * level_of(keys[3], (CELLS,), ((0, 16),), -0.4, 0.0), -1.0, 1.0).astype(jnp.bfloat16)
    rate_matrix = bell_draw(keys[4], (CLASSES, L, L), L ** -0.5, 0.09375, ((0, 16), (1, 16)))
    slope_matrix = bell_draw(keys[5], (CLASSES, L, L), L ** -0.5, 0.09375, ((0, 16), (1, 16)))
    rate_scale = jnp.clip(jnp.exp(math.log(2.0) - 2.3025851 * jax.random.uniform(keys[6], (CLASSES, L), jnp.float32) ** level_of(keys[6], (CLASSES, L), ((0, 16), (1, 16)), -0.2, 0.2)), 0.2, 2.0)
    slope_scale = jnp.clip(jnp.exp(math.log(2.0) - 2.3025851 * jax.random.uniform(keys[7], (CLASSES, L), jnp.float32) ** level_of(keys[7], (CLASSES, L), ((0, 16), (1, 16)), -0.2, 0.2)), 0.2, 2.0)
    return dict(populations=populations, face_speed=face_speed, cell_class=cell_class, class_offset=class_offset, rate_matrix=rate_matrix, slope_matrix=slope_matrix, rate_scale=rate_scale, slope_scale=slope_scale)


cfl_number = 0.4
step_size = 0.5
spread = 1.25


def transport(populations, face_speed):
    padded = jnp.pad(populations, ((1, 1), (0, 0)))
    left = padded[:-1]
    right = padded[1:]
    face_flux = 0.5 * face_speed[:, None] * (left + right) - 0.5 * spread * (right - left)
    return populations + cfl_number * (face_flux[:-1] - face_flux[1:])


def reference(populations, face_speed, cell_class, class_offset, rate_matrix, slope_matrix, rate_scale, slope_scale):
    transported = transport(populations, face_speed)
    narrow = transported.astype(jnp.bfloat16)
    classes = cell_class[:, 0]
    bucket = N_CELLS * CAP

    def one_class(totals, class_id):
        picked = jnp.argsort((classes != class_id).astype(jnp.int32), stable=True)[:bucket].astype(jnp.int32)
        in_class = classes[picked] == class_id
        rows = narrow[picked]
        rate_part = jnp.dot(rows, rate_matrix[class_id].T, preferred_element_type=jnp.float32)
        slope_part = jnp.dot(rows, slope_matrix[class_id].T, preferred_element_type=jnp.float32)
        offsets = class_offset[picked].astype(jnp.float32)[:, None]
        values = rate_scale[class_id][None, :] * rate_part + slope_scale[class_id][None, :] * offsets * slope_part
        values = jnp.where(in_class[:, None], values, jnp.zeros_like(values))
        return totals.at[picked].add(values), None

    start = jnp.zeros(transported.shape, jnp.float32)
    sources, _ = lax.scan(one_class, start, jnp.arange(CLASSES, dtype=jnp.int32))
    updated = transported + step_size * sources
    return sources, updated
```

```python
import functools

import jax
import jax.numpy as jnp
from jax import lax
from jax.experimental import pallas as pl
from jax.experimental.pallas import tpu as pltpu
from jax.sharding import PartitionSpec as P

MESH = pl.DeviceIdType.MESH
F32 = jnp.float32
BF16 = jnp.bfloat16
I32 = jnp.int32

SIDE = 4
RING = 8
LAG = 2


def iota(shape, dim):
    return lax.broadcasted_iota(I32, shape, dim)


def remote(src, dst, send, recv, device):
    return pltpu.make_async_remote_copy(
        src_ref=src, dst_ref=dst, send_sem=send, recv_sem=recv, device_id=device, device_id_type=MESH
    )


def nt(a, b):
    return lax.dot_general(a, b, (((1,), (1,)), ((), ())), preferred_element_type=F32)


def kernel(
    small, pop, rate, slope, rate_gain, slope_gain, sources, updated,
    pad, wr, ws, x, send, off_send, off_recv, back_send, back, pick, moved,
    local_sem, halo_send, halo_recv, out_send, row_recv, offs_recv, ring_recv, pair_recv, back_recv,
):
    rows, width = sources.shape
    groups = SIDE * SIDE
    cap = send.shape[0] // groups
    c = lax.axis_index("cells")
    lev = lax.axis_index("levels")
    cx, cy = lax.div(c, SIDE), lax.rem(c, SIDE)
    z, h = lax.div(lev, 2), lax.rem(lev, 2)
    other = 1 - h
    right = lax.rem(z + 1, RING) * 2 + h
    left = lax.rem(z + RING - 1, RING) * 2 + h
    twin = z * 2 + other
    cell_up = lax.rem(c + 1, groups)
    cell_down = lax.rem(c + groups - 1, groups)

    pop_copy = pltpu.make_async_copy(pop, pad.at[pl.ds(8, rows)], local_sem.at[0])
    rate_copy = pltpu.make_async_copy(rate.at[0], wr, local_sem.at[1])
    slope_copy = pltpu.make_async_copy(slope.at[0], ws, local_sem.at[2])
    pop_copy.start()
    rate_copy.start()
    slope_copy.start()

    def toward(g):
        return lax.rem(cx + SIDE - g // SIDE, SIDE) * SIDE + lax.rem(cy + SIDE - g % SIDE, SIDE)

    def origin(g):
        return lax.rem(cx + lax.div(g, SIDE), SIDE) * SIDE + lax.rem(cy + lax.rem(g, SIDE), SIDE)

    barrier = pltpu.get_barrier_semaphore()
    for g in range(1, groups):
        pl.semaphore_signal(barrier, inc=1, device_id=(toward(g), lev), device_id_type=MESH)
    for peer in (right, left, twin):
        pl.semaphore_signal(barrier, inc=1, device_id=(c, peer), device_id_type=MESH)

    quarter = rows // 4
    cls = jnp.concatenate([small[pl.ds(8 + q, 1), :] for q in range(4)], axis=1).astype(I32)
    hot = (iota((groups, rows), 0) == cls).astype(F32)
    earlier = (iota((rows, rows), 0) < iota((rows, rows), 1)).astype(F32).astype(BF16)
    before = jnp.dot(hot.astype(BF16), earlier, preferred_element_type=F32)
    rank = jnp.sum(hot * before, axis=0, keepdims=True).astype(I32)
    gx = (cx - (cls >> 2)) & (SIDE - 1)
    gy = (cy - (cls & (SIDE - 1))) & (SIDE - 1)
    slot = (gx * SIDE + gy) * cap + rank

    slot4 = jnp.concatenate([slot[:, q * quarter : (q + 1) * quarter] for q in range(4)], axis=0)
    columns = jnp.concatenate([small[...], slot4.astype(F32), jnp.zeros((108, 128), F32)], axis=0).T

    def column(i):
        return columns[:, i : i + 1]

    pop_copy.wait()
    pl.semaphore_wait(barrier, groups - 1 + 3)

    up = remote(
        pad.at[pl.ds(rows, 8)], pad.at[pl.ds(0, 8)], halo_send.at[0], halo_recv.at[0], (cell_up, lev)
    )
    down = remote(
        pad.at[pl.ds(8, 8)], pad.at[pl.ds(rows + 8, 8)], halo_send.at[1], halo_recv.at[1], (cell_down, lev)
    )
    up.start()
    down.start()

    for q in range(4):
        pick[pl.ds(q * quarter, quarter), :] = (
            (iota((quarter, groups * cap), 1) == column(16 + q).astype(I32)).astype(F32).astype(BF16)
        )
    offsets = jnp.concatenate(
        [jnp.broadcast_to(column(12 + q), (quarter, 128)) for q in range(4)], axis=0
    ).astype(BF16)

    up.wait()
    down.wait()

    @pl.when(c == 0)
    def _():
        pad[pl.ds(0, 8), :] = jnp.zeros((8, width), F32)

    @pl.when(c == groups - 1)
    def _():
        pad[pl.ds(rows + 8, 8), :] = jnp.zeros((8, width), F32)

    narrow = []
    for q in range(4):
        a = pad[pl.ds(q * quarter + 7, quarter), :]
        b = pad[pl.ds(q * quarter + 8, quarter), :]
        d = pad[pl.ds(q * quarter + 9, quarter), :]
        lower = 0.5 * column(q) * (a + b) - 0.625 * (b - a)
        upper = 0.5 * column(4 + q) * (b + d) - 0.625 * (d - b)
        t = b + 0.4 * (lower - upper)
        moved[pl.ds(q * quarter, quarter), :] = t
        narrow.append(t.astype(BF16))
    table = jnp.concatenate([jnp.concatenate(narrow, axis=0), offsets], axis=1)

    def rows_of(g):
        return pl.ds(pl.multiple_of(g * cap, cap), cap)

    def row_copy(g, device):
        return remote(
            send.at[rows_of(g)], x.at[h, z, rows_of(g)], out_send.at[0], row_recv.at[g], device
        )

    def off_copy(g, device):
        return remote(
            off_send.at[rows_of(g)], off_recv.at[rows_of(g)], out_send.at[1], offs_recv.at[g], device
        )

    for q in range(4):
        take = (iota((4 * cap, rows), 0) + 4 * cap * q == slot).astype(F32).astype(BF16)
        routed = jnp.dot(take, table, preferred_element_type=F32).astype(BF16)
        if q == 0:
            x[h, z, pl.ds(0, cap), :] = routed[:cap, :width]
            off_recv[pl.ds(0, cap), :] = routed[:cap, width:]
        send[pl.ds(4 * cap * q, 4 * cap), :] = routed[:, :width]
        off_send[pl.ds(4 * cap * q, 4 * cap), :] = routed[:, width:]
        for g in range(max(1, 4 * q), 4 * q + 4):
            row_copy(g, (toward(g), lev)).start()
            off_copy(g, (toward(g), lev)).start()

    rate_copy.wait()
    slope_copy.wait()

    half = cap // 2
    hops = RING // 2

    def ring_copy(g, j, way, device):
        place = lax.rem(z + RING - j, RING) if way == 0 else lax.rem(z + j, RING)
        if j < hops:
            span = rows_of(g)
        else:
            span = pl.ds(pl.multiple_of(g * cap + way * half, half), half)
        return place, span, ring_recv.at[g, way * hops + j - 1], device

    def wait_ring(g, j, way):
        place, span, recv, _ = ring_copy(g, j, way, None)
        ref = x.at[h, place, span]
        remote(ref, ref, out_send.at[2], recv, (c, right)).wait_recv()

    def send_ring(g, j, way):
        if j < hops:
            span = rows_of(g)
        else:
            span = pl.ds(pl.multiple_of(g * cap + way * half, half), half)
        place = lax.rem(z + RING - (j - 1), RING) if way == 0 else lax.rem(z + j - 1, RING)
        ref = x.at[h, place, span]
        remote(
            ref, ref, out_send.at[3 + way * hops + j - 1], ring_recv.at[g, way * hops + j - 1],
            (c, right if way == 0 else left),
        ).start()

    def send_twin(g, place):
        ref = x.at[h, place, rows_of(g)]
        remote(ref, ref, out_send.at[2], pair_recv.at[g], (c, twin)).start()

    def back_copy(g, device):
        return remote(
            back_send.at[rows_of(g)], back.at[rows_of(g)], out_send.at[11], back_recv.at[g], device
        )

    pair = 2 * cap

    def tick(t, carry):
        for j in range(hops, 0, -1):
            g = t - LAG * j

            @pl.when((g >= 0) & (g < groups))
            def _(g=g, j=j):
                for way in range(2):
                    wait_ring(g, j, way)
                    if j < hops:
                        send_ring(g, j + 1, way)
                        send_twin(g, lax.rem(z + RING - j, RING) if way == 0 else lax.rem(z + j, RING))
                if j == hops:
                    send_twin(g, lax.rem(z + hops, RING))

        @pl.when(t < groups)
        def _():
            @pl.when(t > 0)
            def _():
                row_copy(t, (c, lev)).wait_recv()

            for way in range(2):
                send_ring(t, 1, way)
            send_twin(t, z)

        g = t - LAG * (hops + 1)

        @pl.when((g >= 0) & (lax.rem(g + 2, 2) == 1))
        def _():
            for i in range(2):
                span = rows_of(g - 1 + i)
                ref = x.at[other, :, span]
                pltpu.make_async_copy(ref, ref, pair_recv.at[g - 1 + i]).wait()

            @pl.when(g > 1)
            def _():
                off_copy(g - 1, (c, lev)).wait_recv()

            off_copy(g, (c, lev)).wait_recv()
            both = pl.ds(pl.multiple_of((g - 1) * cap, pair), pair)
            rate_part = jnp.zeros((pair, width), F32)
            slope_part = jnp.zeros((pair, width), F32)
            for i in range(2 * RING):
                chunk = x[i // RING, i % RING, both, :]
                lanes = pl.ds((2 * (i % RING) + i // RING) * width, width)
                rate_part += nt(chunk, wr[:, lanes])
                slope_part += nt(chunk, ws[:, lanes])
            o = off_recv[both, :].astype(F32)
            o = jnp.concatenate([o] * (width // 128), axis=1)
            values = rate_gain[...] * rate_part + slope_gain[...] * o * slope_part
            back_send[both, :] = values.astype(BF16)

            @pl.when(g == 1)
            def _():
                back[pl.ds(0, cap), :] = values[:cap].astype(BF16)

            @pl.when(g > 1)
            def _():
                back_copy(g - 1, (origin(g - 1), lev)).start()

            back_copy(g, (origin(g), lev)).start()

        return carry

    lax.fori_loop(0, groups + LAG * (hops + 1), tick, 0)

    total = jnp.zeros((rows, width), F32)
    for q in range(4):
        for g in range(max(1, 4 * q), 4 * q + 4):
            back_copy(g, (c, lev)).wait_recv()
        span = pl.ds(4 * cap * q, 4 * cap)
        total += jnp.dot(pick[:, span], back[span, :], preferred_element_type=F32)
    sources[...] = total
    updated[...] = moved[...] + 0.5 * total

    def drain(ref, sem):
        pltpu.make_async_copy(ref, ref, sem).wait()

    rest = pl.ds(cap, (groups - 1) * cap)
    drain(send.at[rest], out_send.at[0])
    drain(off_send.at[rest], out_send.at[1])
    drain(x.at[0], out_send.at[2])
    for way in range(2):
        for j in range(1, hops):
            drain(x.at[0, 0], out_send.at[3 + way * hops + j - 1])
        drain(x.at[0, 0, pl.ds(0, groups * half)], out_send.at[3 + way * hops + hops - 1])
    drain(back_send.at[rest], out_send.at[11])


def shards(
    populations, face_speed, cell_class, class_offset, rate_matrix, slope_matrix, rate_scale, slope_scale
):
    rows, width = populations.shape
    groups = SIDE * SIDE
    cap = 2 * rows // groups
    slots = groups * cap
    first = lax.axis_index("cells") * rows
    speeds = lax.dynamic_slice_in_dim(face_speed, first, rows + 1)
    small = jnp.concatenate(
        [
            speeds[:-1].reshape(4, -1),
            speeds[1:].reshape(4, -1),
            cell_class.reshape(4, -1).astype(F32),
            class_offset.astype(F32).reshape(4, -1),
        ],
        axis=0,
    )
    vmem = pl.BlockSpec(memory_space=pltpu.VMEM)
    hbm = pl.BlockSpec(memory_space=pl.ANY)
    out = jax.ShapeDtypeStruct((rows, width), F32)
    dma = pltpu.SemaphoreType.DMA
    return pl.pallas_call(
        kernel,
        out_shape=(out, out),
        in_specs=[vmem, hbm, hbm, hbm, vmem, vmem],
        out_specs=(vmem, vmem),
        scratch_shapes=[
            pltpu.VMEM((rows + 16, width), F32),
            pltpu.VMEM(rate_matrix.shape[1:], BF16),
            pltpu.VMEM(slope_matrix.shape[1:], BF16),
            pltpu.VMEM((2, RING, slots, width), BF16),
            pltpu.VMEM((slots, width), BF16),
            pltpu.VMEM((slots, 128), BF16),
            pltpu.VMEM((slots, 128), BF16),
            pltpu.VMEM((slots, width), BF16),
            pltpu.VMEM((slots, width), BF16),
            pltpu.VMEM((rows, slots), BF16),
            pltpu.VMEM((rows, width), F32),
            dma((3,)),
            dma((2,)),
            dma((2,)),
            dma((12,)),
            dma((groups,)),
            dma((groups,)),
            dma((groups, RING)),
            dma((groups,)),
            dma((groups,)),
        ],
        compiler_params=pltpu.CompilerParams(
            collective_id=0, has_side_effects=True, vmem_limit_bytes=60 * 1024 * 1024
        ),
    )(small, populations, rate_matrix, slope_matrix, rate_scale, slope_scale)


def solution(mesh):
    in_specs = (
        P("cells", "levels"),
        P(),
        P("cells", None),
        P("cells"),
        P("cells", "levels", None),
        P("cells", "levels", None),
        P("cells", "levels"),
        P("cells", "levels"),
    )
    out_specs = (P("cells", "levels"), P("cells", "levels"))
    return jax.shard_map(shards, mesh=mesh, in_specs=in_specs, out_specs=out_specs, check_vma=False)
```

```python
import jax
import jax.numpy as jnp
from jax import lax
from jax.experimental import pallas as pl
from jax.experimental.pallas import tpu as pltpu
from jax.sharding import PartitionSpec as P

MESH = pl.DeviceIdType.MESH
F32 = jnp.float32
BF16 = jnp.bfloat16
I32 = jnp.int32

SIDE = 4
RING = 8
HOPS = RING // 2


def iota(shape, dim):
    return lax.broadcasted_iota(I32, shape, dim)


def remote(src, dst, send, recv, device):
    return pltpu.make_async_remote_copy(
        src_ref=src, dst_ref=dst, send_sem=send, recv_sem=recv, device_id=device, device_id_type=MESH
    )


def nt(a, b):
    return lax.dot_general(a, b, (((1,), (1,)), ((), ())), preferred_element_type=F32)


def steps_of(g):
    i, j = g // SIDE, g % SIDE
    j = j + (i // 2) * (SIDE - 1 - 2 * j)
    return (i % 2) * 2 + i // 2, j + j // 2 - 2 * (j // 3)


def kernel(
    cls4, off4, speeds, pop, rate, slope, rate_gain, slope_gain, sources, transported,
    pad, wr, ws, x, flat, send, off_send, off_recv, back_send, back, take, pick, moved, acc, result,
    local_sem, halo_send, halo_recv, out_send, row_recv, many_recv, offs_recv, ring_recv, flat_recv,
    padded_twin, flat_twin, back_recv,
):
    rows, width = result.shape
    groups = SIDE * SIDE
    cap = back.shape[0] // groups
    batch = groups // 2
    quarter = rows // 4
    c = lax.axis_index("cells")
    lev = lax.axis_index("levels")
    cx, cy = lax.div(c, SIDE), lax.rem(c, SIDE)
    z, h = lax.div(lev, 2), lax.rem(lev, 2)
    right = lax.rem(z + 1, RING) * 2 + h
    left = lax.rem(z + RING - 1, RING) * 2 + h
    twin = z * 2 + 1 - h
    cell_up = lax.rem(c + 1, groups)
    cell_down = lax.rem(c + groups - 1, groups)

    barrier = pltpu.get_barrier_semaphore()

    def toward(g):
        dx, dy = steps_of(g)
        return lax.rem(cx + SIDE - dx, SIDE) * SIDE + lax.rem(cy + SIDE - dy, SIDE)

    def origin(g):
        i, j = lax.div(g, SIDE), lax.rem(g, SIDE)
        j = j + lax.div(i, 2) * (SIDE - 1 - 2 * j)
        dx = lax.rem(i, 2) * 2 + lax.div(i, 2)
        dy = j + lax.div(j, 2) - 2 * lax.div(j, 3)
        return lax.rem(cx + dx, SIDE) * SIDE + lax.rem(cy + dy, SIDE)

    for g in range(1, groups):
        pl.semaphore_signal(barrier, inc=1, device_id=(toward(g), lev), device_id_type=MESH)
    for peer in (right, left, twin):
        pl.semaphore_signal(barrier, inc=1, device_id=(c, peer), device_id_type=MESH)

    pop_copy = pltpu.make_async_copy(pop, pad.at[pl.ds(8, rows)], local_sem.at[0])
    pop_copy.start()
    for i in range(2 * RING):
        lanes = pl.ds(i * width, width)
        pltpu.make_async_copy(rate.at[0, :, lanes], wr.at[i], local_sem.at[1]).start()
        pltpu.make_async_copy(slope.at[0, :, lanes], ws.at[i], local_sem.at[2]).start()

    cls = jnp.concatenate([cls4[pl.ds(q, 1), :] for q in range(4)], axis=1)
    hot = (iota((groups, rows), 0) == cls).astype(F32)
    earlier = (iota((rows, rows), 0) < iota((rows, rows), 1)).astype(F32).astype(BF16)
    before = jnp.dot(hot.astype(BF16), earlier, preferred_element_type=F32)
    rank = jnp.sum(hot * before, axis=0, keepdims=True).astype(I32)
    dx = (cx - (cls >> 2)) & (SIDE - 1)
    dy = (cy - (cls & (SIDE - 1))) & (SIDE - 1)
    i, j = (dx & 1) * 2 + (dx >> 1), dy ^ (dy >> 1)
    j = j + (i >> 1) * (SIDE - 1 - 2 * j)
    slot = (i * SIDE + j) * cap + rank

    slot4 = jnp.concatenate([slot[:, q * quarter : (q + 1) * quarter] for q in range(4)], axis=0)
    base = pl.multiple_of(c * rows, rows)
    line = [speeds[pl.ds(base + q * quarter, quarter)].reshape(1, quarter) for q in range(4)]
    end = speeds[pl.ds(base + rows, 1)].reshape(1, 1)
    line = jnp.concatenate(line + [jnp.broadcast_to(end, (1, quarter))], axis=1)
    ahead = pltpu.roll(line, 5 * quarter - 1, 1)
    o4 = off4[...].astype(F32).reshape(4, quarter)
    columns = jnp.concatenate(
        [line[:, q * quarter : (q + 1) * quarter] for q in range(4)] +
        [ahead[:, q * quarter : (q + 1) * quarter] for q in range(4)] +
        [slot4.astype(F32), jnp.zeros((116, 128), F32)], axis=0
    ).T

    def column(i):
        return columns[:, i : i + 1]

    pop_copy.wait()
    pl.semaphore_wait(barrier, groups - 1 + 3)

    up = remote(
        pad.at[pl.ds(rows, 8)], pad.at[pl.ds(0, 8)], halo_send.at[0], halo_recv.at[0], (cell_up, lev)
    )
    down = remote(
        pad.at[pl.ds(8, 8)], pad.at[pl.ds(rows + 8, 8)], halo_send.at[1], halo_recv.at[1], (cell_down, lev)
    )
    up.start()
    down.start()

    for q in range(4):
        take[pl.ds(4 * cap * q, 4 * cap), :] = (
            (iota((4 * cap, rows), 0) + 4 * cap * q == slot).astype(F32).astype(BF16)
        )

    up.wait()
    down.wait()

    @pl.when(c == 0)
    def _():
        pad[pl.ds(0, 8), :] = jnp.zeros((8, width), F32)

    @pl.when(c == groups - 1)
    def _():
        pad[pl.ds(rows + 8, 8), :] = jnp.zeros((8, width), F32)

    for q in range(4):
        a = pad[pl.ds(q * quarter + 7, quarter), :]
        b = pad[pl.ds(q * quarter + 8, quarter), :]
        d = pad[pl.ds(q * quarter + 9, quarter), :]
        lower = 0.5 * column(q) * (a + b) - 0.625 * (b - a)
        upper = 0.5 * column(4 + q) * (b + d) - 0.625 * (d - b)
        t = b + 0.4 * (lower - upper)
        moved[pl.ds(q * quarter, quarter), :] = t
        flat[z, pl.ds(q * quarter, quarter), :] = t.astype(BF16)

    offsets = jnp.broadcast_to(
        jnp.concatenate([o4[q : q + 1] for q in range(4)], axis=1), (16, rows)
    ).astype(BF16)
    moved_copy = pltpu.make_async_copy(moved, transported, local_sem.at[0])

    half = cap // 2
    near = batch // 2
    pieces = 4
    piece = rows // pieces
    offset = (0, -1, 1, -2, 2, -3, 3, HOPS)

    def rows_of(g):
        return pl.ds(pl.multiple_of(g * cap, cap), cap)

    def place_at(i):
        return lax.rem(z + RING + i, RING)

    def place_of(j, way):
        return place_at(-j if way == 0 else j)

    def toward_way(way):
        return (c, right if way == 0 else left)

    def each(lower, upper, f):
        def body(g, carry):
            f(g)
            return carry

        lax.fori_loop(lower, upper, body, 0)

    def route(place, b, own_role):
        for q in range(2):
            span = pl.ds((b * batch + q * near) * cap, near * cap)
            got = jnp.dot(take[span, :], flat[place], preferred_element_type=F32).astype(BF16)
            send[place, span, :] = got
            if b == 0 and q == 0:
                x[own_role, place, pl.ds(0, cap), :] = got[:cap]

    def off_copy(g, device):
        return remote(off_send.at[g // 2], off_recv.at[g], out_send.at[1], offs_recv.at[g], device)

    def send_offsets():
        got = nt(offsets, take[...]).astype(BF16)
        for p in range(batch):
            off_send[p] = got[:, 2 * cap * p : 2 * cap * (p + 1)]
        off_recv[0] = got[:, : 2 * cap]
        for g in range(1, groups):
            off_copy(g, (toward(g), lev)).start()

    def make_pick():
        for q in range(4):
            pick[pl.ds(q * quarter, quarter), :] = (
                (iota((quarter, groups * cap), 1) == column(8 + q).astype(I32)).astype(F32).astype(BF16)
            )

    def wait_bytes(ref, sem):
        pltpu.make_async_copy(ref, ref, sem).wait()

    def wait_weights():
        wait_bytes(wr, local_sem.at[1])
        wait_bytes(ws, local_sem.at[2])

    def multiply(b, role, shift, start=0, count=batch, fresh=False):
        place = place_at(shift)
        level = place * 2 + role
        span = pl.ds((b * batch + start) * cap, count * cap)
        chunk = x[role, place, span, :]
        for n, w in ((0, wr), (1, ws)):
            part = nt(chunk, w[level])
            acc[n, span, :] = part if fresh else acc[n, span, :] + part

    def multiply_two(b, role, j):
        each(0, 2, lambda i: multiply(b, role, j * (2 * i - 1)))

    def when(i, at, f):
        pl.when(i == at)(f)

    def back_copy(g, device):
        return remote(
            back_send.at[rows_of(g)], back.at[rows_of(g)], out_send.at[3], back_recv.at[g], device
        )

    def finish(b, start, count):
        base = b * batch + start
        for g in range(max(1, base), base + count):
            off_copy(g, (c, lev)).wait_recv()
        low = iota((1, 2 * cap), 1) < cap
        o = [
            jnp.where(low, off_recv[g, 0:1, :].astype(F32), off_recv[g + 1, 0:1, :].astype(F32))
            for g in range(base, base + count, 2)
        ]
        o = jnp.concatenate(o + [jnp.zeros((128 - len(o), 2 * cap), F32)], axis=0).T
        for p in range(count // 2):
            two = pl.ds((base + 2 * p) * cap, 2 * cap)
            values = rate_gain[...] * acc[0, two, :] + slope_gain[...] * o[:, p : p + 1] * acc[1, two, :]
            back_send[two, :] = values.astype(BF16)
            if base + p == 0:
                back[pl.ds(0, cap), :] = values[:cap].astype(BF16)
        for g in range(max(1, base), base + count):
            back_copy(g, (origin(g), lev)).start()

    def collect(base, count):
        for g in range(max(1, base), base + count):
            back_copy(g, (c, lev)).wait_recv()
        span = pl.ds(base * cap, count * cap)
        return jnp.dot(pick[:, span], back[span, :], preferred_element_type=F32)

    def wait_padded(number, chunks, start, count):
        wait_bytes(x.at[0, pl.ds(0, chunks), pl.ds(start * cap, count * cap)], padded_twin.at[number])

    def wait_flat(number, count=batch):
        wait_bytes(x.at[1, 0, pl.ds(0, count * cap)], flat_twin.at[number])

    @pl.when(h == 0)
    def _():
        def row_copy(g, device):
            return remote(
                send.at[z, rows_of(g)], x.at[0, z, rows_of(g)], out_send.at[0], row_recv.at[g], device
            )

        def span_of(g, j, way):
            if j < HOPS:
                return rows_of(g)
            return pl.ds(pl.multiple_of(g * cap + way * half, half), half)

        def ring_ref(g, j, way, place):
            return x.at[0, place, span_of(g, j, way)]

        def wait_ring(g, j, way):
            ref = ring_ref(g, j, way, place_of(j, way))
            recv = ring_recv.at[g, way * HOPS + j - 1]
            remote(ref, ref, out_send.at[2], recv, toward_way(way)).wait_recv()

        def send_ring(g, j, way):
            ref = ring_ref(g, j, way, place_of(j - 1, way))
            recv = ring_recv.at[g, way * HOPS + j - 1]
            remote(ref, ref, out_send.at[4 if j < HOPS else 5], recv, toward_way(way)).start()

        def send_twin(g, place, number):
            ref = x.at[0, place, rows_of(g)]
            remote(ref, ref, out_send.at[2], padded_twin.at[number], (c, twin)).start()

        def first(g, b):
            if not isinstance(g, int):
                row_copy(g, (c, lev)).wait_recv()

            for way in range(2):
                send_ring(g, 1, way)
            send_twin(g, z, 5 * b)

        def middle(g, b, j):
            for way in range(2):
                wait_ring(g, j, way)
                send_ring(g, j + 1, way)
                send_twin(g, place_of(j, way), 5 * b + j)

        def last(g, number):
            for way in range(2):
                wait_ring(g, HOPS, way)
            send_twin(g, place_of(HOPS, 0), number)

        def send_rows(b):
            route(z, b, 0)
            for g in range(max(1, b * batch), (b + 1) * batch):
                row_copy(g, (toward(g), lev)).start()

        send_rows(0)
        first(0, 0)
        make_pick()
        moved_copy.start()
        each(1, near, lambda g: first(g, 0))

        def start_up(g):
            first(g + near, 0)
            middle(g, 0, 1)

        each(0, near, start_up)
        send_rows(1)
        send_offsets()
        each(near, batch, lambda g: middle(g, 0, 1))
        wait_weights()
        multiply(0, 0, 0, fresh=True)

        def turn_2(i):
            middle(i, 0, 2)
            when(i, 1, lambda: multiply(0, 0, -1))
            when(i, 3, lambda: multiply(0, 0, 1))

        each(0, batch, turn_2)

        def turn_3(i):
            middle(i, 0, 3)
            when(i, 1, lambda: multiply(0, 0, -2))
            when(i, 3, lambda: multiply(0, 0, 2))

            @pl.when(i == 5)
            def _():
                wait_flat(0)
                multiply(0, 1, 0)

        each(0, batch, turn_3)
        each(batch, groups, lambda g: first(g, 1))

        def turn_last(i):
            last(i, HOPS)
            when(i, 1, lambda: multiply(0, 0, -3))
            when(i, 2, lambda: multiply(0, 0, 3))

            @pl.when(i == 4)
            def _():
                wait_flat(1)
                multiply(0, 1, -1)

            @pl.when(i == 6)
            def _():
                wait_flat(2)
                multiply(0, 1, 1)

        each(0, batch, turn_last)

        def turn_over(i):
            middle(batch + i, 1, 1)
            when(i, 0, lambda: multiply(0, 0, HOPS))

            @pl.when(i == 2)
            def _():
                wait_flat(3)
                multiply(0, 1, -2)

            @pl.when(i == 4)
            def _():
                wait_flat(4)
                multiply(0, 1, 2)

            when(i, 6, lambda: multiply(1, 0, 0, fresh=True))

        each(0, batch, turn_over)

        def turn_6(i):
            middle(batch + i, 1, 2)

            @pl.when(i == 0)
            def _():
                wait_flat(5)
                multiply(0, 1, -3)

            @pl.when(i == 2)
            def _():
                wait_flat(6)
                multiply(0, 1, 3)

            @pl.when(i == 4)
            def _():
                wait_flat(7)
                multiply(0, 1, HOPS)
                finish(0, 0, batch)

            when(i, 5, lambda: multiply(1, 0, -1))
            when(i, 6, lambda: multiply(1, 0, 1))

        each(0, batch, turn_6)

        def turn_7(i):
            middle(batch + i, 1, 3)

            @pl.when(i == 0)
            def _():
                wait_flat(8)
                multiply(1, 1, 0)

            when(i, 1, lambda: multiply(1, 0, -2))
            when(i, 2, lambda: multiply(1, 0, 2))

            @pl.when(i == 4)
            def _():
                wait_flat(9)
                multiply(1, 1, -1)

            @pl.when(i == 6)
            def _():
                wait_flat(10)
                multiply(1, 1, 1)

        each(0, batch, turn_7)
        each(0, 2, lambda i: multiply(1, 0, 3 * (2 * i - 1)))
        each(batch, batch + near, lambda g: last(g, 5 + HOPS))
        each(batch + near, groups, lambda g: last(g, 5 + HOPS + 1))
        multiply(1, 0, HOPS)
        wait_flat(11)
        multiply(1, 1, -2)
        wait_flat(12)
        multiply(1, 1, 2)
        result[...] = collect(0, batch)
        wait_flat(13)
        multiply(1, 1, -3)
        wait_flat(14)
        multiply(1, 1, 3)
        for s in range(2):
            wait_flat(15 + s, near)
            multiply(1, 1, HOPS, s * near, near)
            finish(1, s * near, near)

    @pl.when(h == 1)
    def _():
        def number_of(b, i, s):
            return i if b == 0 else batch + i + s

        def flat_ref(p, j, way, place):
            if j < HOPS:
                return flat.at[place, pl.ds(p * piece, piece)]
            return flat.at[place, pl.ds(p * piece + way * (piece // 2), piece // 2)]

        def send_flat(p, j, way):
            ref = flat_ref(p, j, way, place_of(j - 1, way))
            recv = flat_recv.at[p, way * HOPS + j - 1]
            remote(ref, ref, out_send.at[4 if j < HOPS else 5], recv, toward_way(way)).start()

        def hop(j):
            for p in range(pieces):
                for way in range(2):
                    ref = flat_ref(p, j, way, place_of(j, way))
                    recv = flat_recv.at[p, way * HOPS + j - 1]
                    remote(ref, ref, out_send.at[4], recv, toward_way(way)).wait_recv()
                    if j < HOPS:
                        send_flat(p, j + 1, way)

        def send_rows(b, i):
            place = place_at(offset[i])
            for g in range(max(1, b * batch), (b + 1) * batch):
                recv = many_recv.at[number_of(b, i, (g - batch) // near if b == 1 and i == RING - 1 else 0)]
                remote(
                    send.at[place, rows_of(g)], x.at[1, place, rows_of(g)], out_send.at[0], recv,
                    (toward(g), lev),
                ).start()

        def arrived(b, i, s=None):
            place = place_at(offset[i])
            start, count = (b * batch, batch) if s is None else (b * batch + s * near, near)
            number = number_of(b, i, s or 0)
            base = max(1, start)
            wait_bytes(
                x.at[1, place, pl.ds(base * cap, (start + count - base) * cap)], many_recv.at[number]
            )
            ref = x.at[1, place, pl.ds(start * cap, count * cap)]
            remote(ref, ref, out_send.at[2], flat_twin.at[number], (c, twin)).start()

        for p in range(pieces):
            for way in range(2):
                send_flat(p, 1, way)
        def pass_on(b, *numbers):
            for i in numbers:
                route(place_at(offset[i]), b, 1)
                send_rows(b, i)

        pass_on(0, 0)
        make_pick()
        moved_copy.start()
        hop(1)
        pass_on(0, 1, 2)
        pass_on(1, 0)
        send_offsets()
        arrived(0, 0)
        wait_weights()
        multiply(0, 1, 0, fresh=True)
        hop(2)
        pass_on(0, 3, 4)
        pass_on(1, 1)
        arrived(0, 1)
        arrived(0, 2)
        multiply_two(0, 1, 1)
        hop(3)
        pass_on(0, 5, 6)
        pass_on(1, 2)
        arrived(0, 3)
        arrived(0, 4)
        wait_padded(0, 1, 0, batch)
        multiply(0, 0, 0)
        hop(HOPS)
        pass_on(0, 7)
        pass_on(1, 3, 4)
        arrived(0, 5)
        arrived(0, 6)
        pass_on(1, 5, 6)
        multiply_two(0, 1, 2)
        pass_on(1, 7)
        wait_padded(1, 2, 0, batch)
        multiply_two(0, 0, 1)
        arrived(0, 7)
        multiply_two(0, 1, 3)
        arrived(1, 0)
        wait_padded(2, 2, 0, batch)
        multiply_two(0, 0, 2)
        multiply(0, 1, HOPS)
        arrived(1, 1)
        arrived(1, 2)
        wait_padded(3, 2, 0, batch)
        multiply_two(0, 0, 3)
        wait_padded(HOPS, 1, 0, batch)
        multiply(0, 0, HOPS)
        finish(0, 0, batch)
        multiply(1, 1, 0, fresh=True)
        for i in (3, 4):
            arrived(1, i)
        multiply_two(1, 1, 1)
        wait_padded(5, 1, batch, batch)
        multiply(1, 0, 0)
        for i in (5, 6):
            arrived(1, i)
        multiply_two(1, 1, 2)
        arrived(1, RING - 1, 0)
        wait_padded(6, 2, batch, batch)
        multiply_two(1, 0, 1)
        arrived(1, RING - 1, 1)
        multiply_two(1, 1, 3)
        wait_padded(7, 2, batch, batch)
        multiply_two(1, 0, 2)
        multiply(1, 1, HOPS)
        result[...] = collect(0, batch)
        wait_padded(8, 2, batch, batch)
        multiply_two(1, 0, 3)
        for s in range(2):
            wait_padded(5 + HOPS + s, 1, batch + s * near, near)
            multiply(1, 0, HOPS, s * near, near)
            finish(1, s * near, near)

    result[...] += collect(batch, near)
    total = result[...] + collect(batch + near, near)
    sources[...] = total.astype(BF16)

    moved_copy.wait()
    rest = pl.ds(cap, (groups - 1) * cap)

    @pl.when(h == 0)
    def _():
        wait_bytes(send.at[0, rest], out_send.at[0])
        wait_bytes(x.at[0, pl.ds(0, 2 * HOPS - 2)], out_send.at[4])
        wait_bytes(x.at[0, 0], out_send.at[5])

    @pl.when(h == 1)
    def _():
        wait_bytes(send.at[:, rest], out_send.at[0])
        wait_bytes(flat.at[pl.ds(0, 2 * HOPS - 2)], out_send.at[4])
        wait_bytes(flat.at[0], out_send.at[5])

    wait_bytes(off_recv.at[pl.ds(1, groups - 1)], out_send.at[1])
    wait_bytes(x.at[0], out_send.at[2])
    wait_bytes(back_send.at[rest], out_send.at[3])


def shards(
    populations, face_speed, cell_class, class_offset, rate_matrix, slope_matrix, rate_scale, slope_scale
):
    rows, width = populations.shape
    groups = SIDE * SIDE
    cap = 2 * rows // groups
    slots = groups * cap
    vmem = pl.BlockSpec(memory_space=pltpu.VMEM)
    hbm = pl.BlockSpec(memory_space=pl.ANY)
    dma = pltpu.SemaphoreType.DMA
    narrow_sources, transported = pl.pallas_call(
        kernel,
        out_shape=(
            jax.ShapeDtypeStruct((rows, width), BF16), jax.ShapeDtypeStruct((rows, width), F32)
        ),
        in_specs=[vmem, vmem, vmem, hbm, hbm, hbm, vmem, vmem],
        out_specs=(vmem, hbm),
        scratch_shapes=[
            pltpu.VMEM((rows + 16, width), F32),
            pltpu.VMEM((2 * RING, width, width), BF16),
            pltpu.VMEM((2 * RING, width, width), BF16),
            pltpu.VMEM((2, RING, slots, width), BF16),
            pltpu.VMEM((RING, rows, width), BF16),
            pltpu.VMEM((RING, slots, width), BF16),
            pltpu.VMEM((groups // 2, 16, 128), BF16),
            pltpu.VMEM((groups, 16, 128), BF16),
            pltpu.VMEM((slots, width), BF16),
            pltpu.VMEM((slots, width), BF16),
            pltpu.VMEM((slots, rows), BF16),
            pltpu.VMEM((rows, slots), BF16),
            pltpu.VMEM((rows, width), F32),
            pltpu.VMEM((2, slots, width), F32),
            pltpu.VMEM((rows, width), F32),
            dma((3,)),
            dma((2,)),
            dma((2,)),
            dma((6,)),
            dma((groups,)),
            dma((2 * RING + 1,)),
            dma((groups,)),
            dma((groups, RING)),
            dma((4, RING)),
            dma((11,)),
            dma((2 * RING + 1,)),
            dma((groups,)),
        ],
        compiler_params=pltpu.CompilerParams(
            collective_id=0, has_side_effects=True, vmem_limit_bytes=60 * 1024 * 1024
        ),
    )(
        cell_class.reshape(4, -1), class_offset, face_speed,
        populations, rate_matrix, slope_matrix, rate_scale, slope_scale,
    )
    sources = narrow_sources.astype(F32)
    return sources, transported + 0.5 * sources


def solution(mesh):
    in_specs = (
        P("cells", "levels"),
        P(),
        P("cells", None),
        P("cells"),
        P("cells", "levels", None),
        P("cells", "levels", None),
        P("cells", "levels"),
        P("cells", "levels"),
    )
    out_specs = (P("cells", "levels"), P("cells", "levels"))
    return jax.shard_map(shards, mesh=mesh, in_specs=in_specs, out_specs=out_specs, check_vma=False)
```

```python
import jax
import jax.numpy as jnp
from jax import lax
from jax.experimental import pallas as pl
from jax.experimental.pallas import tpu as pltpu
from jax.sharding import PartitionSpec as P

MESH = pl.DeviceIdType.MESH
F32 = jnp.float32
BF16 = jnp.bfloat16
I32 = jnp.int32

SIDE = 4
RING = 8
HOPS = RING // 2


def iota(shape, dim):
    return lax.broadcasted_iota(I32, shape, dim)


def remote(src, dst, send, recv, device):
    return pltpu.make_async_remote_copy(
        src_ref=src, dst_ref=dst, send_sem=send, recv_sem=recv, device_id=device, device_id_type=MESH
    )


def nt(a, b):
    return lax.dot_general(a, b, (((1,), (1,)), ((), ())), preferred_element_type=F32)


def steps_of(g):
    i, j = g // SIDE, g % SIDE
    j = j + (i // 2) * (SIDE - 1 - 2 * j)
    return (i % 2) * 2 + i // 2, j + j // 2 - 2 * (j // 3)


def kernel(
    cls_in, off_in, speeds_in, pop, rate, slope, rate_gain_in, slope_gain_in, sources, transported,
    cls4, off4, speeds, rate_gain, slope_gain, pad, wr, ws, x, flat, send, off_send, off_recv, back_send, back, take, pick, moved, acc, result,
    local_sem, halo_send, halo_recv, out_send, row_recv, many_recv, offs_recv, ring_recv, flat_recv,
    padded_twin, flat_twin, back_recv,
):
    rows, width = result.shape
    groups = SIDE * SIDE
    cap = back.shape[0] // groups
    batch = groups // 2
    quarter = rows // 4
    c = lax.axis_index("cells")
    lev = lax.axis_index("levels")
    cx, cy = lax.div(c, SIDE), lax.rem(c, SIDE)
    z, h = lax.div(lev, 2), lax.rem(lev, 2)
    right = lax.rem(z + 1, RING) * 2 + h
    left = lax.rem(z + RING - 1, RING) * 2 + h
    twin = z * 2 + 1 - h
    cell_up = lax.rem(c + 1, groups)
    cell_down = lax.rem(c + groups - 1, groups)

    barrier = pltpu.get_barrier_semaphore()

    def toward(g):
        dx, dy = steps_of(g)
        return lax.rem(cx + SIDE - dx, SIDE) * SIDE + lax.rem(cy + SIDE - dy, SIDE)

    def origin(g):
        i, j = lax.div(g, SIDE), lax.rem(g, SIDE)
        j = j + lax.div(i, 2) * (SIDE - 1 - 2 * j)
        dx = lax.rem(i, 2) * 2 + lax.div(i, 2)
        dy = j + lax.div(j, 2) - 2 * lax.div(j, 3)
        return lax.rem(cx + dx, SIDE) * SIDE + lax.rem(cy + dy, SIDE)

    for g in range(1, groups):
        pl.semaphore_signal(barrier, inc=1, device_id=(toward(g), lev), device_id_type=MESH)
    for peer in (right, left, twin):
        pl.semaphore_signal(barrier, inc=1, device_id=(c, peer), device_id_type=MESH)

    pop_copy = pltpu.make_async_copy(pop, pad.at[pl.ds(8, rows)], local_sem.at[0])
    small = [
        pltpu.make_async_copy(src, dst, local_sem.at[3 + i])
        for i, (src, dst) in enumerate((
            (cls_in, cls4), (off_in, off4), (speeds_in, speeds),
            (rate_gain_in, rate_gain), (slope_gain_in, slope_gain),
        ))
    ]
    for copy in small[:3]:
        copy.start()
    pop_copy.start()
    for copy in small[3:]:
        copy.start()
    for i in range(2 * RING):
        lanes = pl.ds(i * width, width)
        pltpu.make_async_copy(rate.at[0, :, lanes], wr.at[i], local_sem.at[1]).start()
        pltpu.make_async_copy(slope.at[0, :, lanes], ws.at[i], local_sem.at[2]).start()

    for copy in small[:3]:
        copy.wait()
    cls = jnp.concatenate([cls4[pl.ds(q, 1), :] for q in range(4)], axis=1)
    hot = (iota((groups, rows), 0) == cls).astype(F32)
    earlier = (iota((rows, rows), 0) < iota((rows, rows), 1)).astype(F32).astype(BF16)
    before = jnp.dot(hot.astype(BF16), earlier, preferred_element_type=F32)
    rank = jnp.sum(hot * before, axis=0, keepdims=True).astype(I32)
    dx = (cx - (cls >> 2)) & (SIDE - 1)
    dy = (cy - (cls & (SIDE - 1))) & (SIDE - 1)
    i, j = (dx & 1) * 2 + (dx >> 1), dy ^ (dy >> 1)
    j = j + (i >> 1) * (SIDE - 1 - 2 * j)
    slot = (i * SIDE + j) * cap + rank

    slot4 = jnp.concatenate([slot[:, q * quarter : (q + 1) * quarter] for q in range(4)], axis=0)
    base = pl.multiple_of(c * rows, rows)
    line = [speeds[pl.ds(base + q * quarter, quarter)].reshape(1, quarter) for q in range(4)]
    end = speeds[pl.ds(base + rows, 1)].reshape(1, 1)
    line = jnp.concatenate(line + [jnp.broadcast_to(end, (1, quarter))], axis=1)
    ahead = pltpu.roll(line, 5 * quarter - 1, 1)
    o4 = off4[...].astype(F32).reshape(4, quarter)
    columns = jnp.concatenate(
        [line[:, q * quarter : (q + 1) * quarter] for q in range(4)] +
        [ahead[:, q * quarter : (q + 1) * quarter] for q in range(4)] +
        [slot4.astype(F32), jnp.zeros((116, 128), F32)], axis=0
    ).T

    def column(i):
        return columns[:, i : i + 1]

    pop_copy.wait()
    pl.semaphore_wait(barrier, groups - 1 + 3)

    up = remote(
        pad.at[pl.ds(rows, 8)], pad.at[pl.ds(0, 8)], halo_send.at[0], halo_recv.at[0], (cell_up, lev)
    )
    down = remote(
        pad.at[pl.ds(8, 8)], pad.at[pl.ds(rows + 8, 8)], halo_send.at[1], halo_recv.at[1], (cell_down, lev)
    )
    up.start()
    down.start()

    for q in range(4):
        take[pl.ds(4 * cap * q, 4 * cap), :] = (
            (iota((4 * cap, rows), 0) + 4 * cap * q == slot).astype(F32).astype(BF16)
        )

    def transport(start, count):
        q, r = start // quarter, start % quarter
        a = pad[pl.ds(start + 7, count), :]
        b = pad[pl.ds(start + 8, count), :]
        d = pad[pl.ds(start + 9, count), :]
        lower = 0.5 * column(q)[r : r + count] * (a + b) - 0.625 * (b - a)
        upper = 0.5 * column(4 + q)[r : r + count] * (b + d) - 0.625 * (d - b)
        t = b + 0.4 * (lower - upper)
        moved[pl.ds(start, count), :] = t
        flat[z, pl.ds(start, count), :] = t.astype(BF16)

    edge = 16
    transport(edge, quarter - edge)
    transport(quarter, quarter)
    transport(2 * quarter, quarter)
    transport(3 * quarter, quarter - edge)
    up.wait()
    down.wait()

    @pl.when(c == 0)
    def _():
        pad[pl.ds(0, 8), :] = jnp.zeros((8, width), F32)

    @pl.when(c == groups - 1)
    def _():
        pad[pl.ds(rows + 8, 8), :] = jnp.zeros((8, width), F32)

    transport(0, edge)
    transport(rows - edge, edge)

    offsets = jnp.broadcast_to(
        jnp.concatenate([o4[q : q + 1] for q in range(4)], axis=1), (16, rows)
    ).astype(BF16)
    moved_copy = pltpu.make_async_copy(moved, transported, local_sem.at[0])

    half = cap // 2
    near = batch // 2
    pieces = 4
    piece = rows // pieces
    offset = (0, -1, 1, -2, 2, -3, 3, HOPS)

    def rows_of(g):
        return pl.ds(pl.multiple_of(g * cap, cap), cap)

    def place_at(i):
        return lax.rem(z + RING + i, RING)

    def place_of(j, way):
        return place_at(-j if way == 0 else j)

    def toward_way(way):
        return (c, right if way == 0 else left)

    def each(lower, upper, f):
        def body(g, carry):
            f(g)
            return carry

        lax.fori_loop(lower, upper, body, 0)

    def route(place, b, own_role):
        for q in range(2):
            span = pl.ds((b * batch + q * near) * cap, near * cap)
            got = jnp.dot(take[span, :], flat[place], preferred_element_type=F32).astype(BF16)
            send[place, span, :] = got
            if b == 0 and q == 0:
                x[own_role, place, pl.ds(0, cap), :] = got[:cap]

    def off_copy(g, device):
        return remote(off_send.at[g // 2], off_recv.at[g], out_send.at[1], offs_recv.at[g], device)

    def send_offsets():
        got = nt(offsets, take[...]).astype(BF16)
        for p in range(batch):
            off_send[p] = got[:, 2 * cap * p : 2 * cap * (p + 1)]
        off_recv[0] = got[:, : 2 * cap]
        for g in range(1, groups):
            off_copy(g, (toward(g), lev)).start()

    def make_pick():
        for q in range(4):
            pick[pl.ds(q * quarter, quarter), :] = (
                (iota((quarter, groups * cap), 1) == column(8 + q).astype(I32)).astype(F32).astype(BF16)
            )

    def wait_bytes(ref, sem):
        pltpu.make_async_copy(ref, ref, sem).wait()

    def wait_weights():
        wait_bytes(wr, local_sem.at[1])
        wait_bytes(ws, local_sem.at[2])
        for copy in small[3:]:
            copy.wait()

    def multiply(b, role, shift, start=0, count=batch, fresh=False):
        place = place_at(shift)
        level = place * 2 + role
        span = pl.ds((b * batch + start) * cap, count * cap)
        chunk = x[role, place, span, :]
        for n, w in ((0, wr), (1, ws)):
            part = nt(chunk, w[level])
            acc[n, span, :] = part if fresh else acc[n, span, :] + part

    def multiply_two(b, role, j):
        each(0, 2, lambda i: multiply(b, role, j * (2 * i - 1)))

    def when(i, at, f):
        pl.when(i == at)(f)

    def back_copy(g, device):
        return remote(
            back_send.at[rows_of(g)], back.at[rows_of(g)], out_send.at[3], back_recv.at[g], device
        )

    def finish(b, start, count):
        base = b * batch + start
        for g in range(max(1, base), base + count):
            off_copy(g, (c, lev)).wait_recv()
        low = iota((1, 2 * cap), 1) < cap
        o = [
            jnp.where(low, off_recv[g, 0:1, :].astype(F32), off_recv[g + 1, 0:1, :].astype(F32))
            for g in range(base, base + count, 2)
        ]
        o = jnp.concatenate(o + [jnp.zeros((128 - len(o), 2 * cap), F32)], axis=0).T
        for p in range(count // 2):
            two = pl.ds((base + 2 * p) * cap, 2 * cap)
            values = rate_gain[...] * acc[0, two, :] + slope_gain[...] * o[:, p : p + 1] * acc[1, two, :]
            back_send[two, :] = values.astype(BF16)
            if base + p == 0:
                back[pl.ds(0, cap), :] = values[:cap].astype(BF16)
        for g in range(max(1, base), base + count):
            back_copy(g, (origin(g), lev)).start()

    def collect(base, count):
        for g in range(max(1, base), base + count):
            back_copy(g, (c, lev)).wait_recv()
        span = pl.ds(base * cap, count * cap)
        return jnp.dot(pick[:, span], back[span, :], preferred_element_type=F32)

    def wait_padded(number, chunks, start, count):
        wait_bytes(x.at[0, pl.ds(0, chunks), pl.ds(start * cap, count * cap)], padded_twin.at[number])

    def wait_flat(number, count=batch):
        wait_bytes(x.at[1, 0, pl.ds(0, count * cap)], flat_twin.at[number])

    @pl.when(h == 0)
    def _():
        def row_copy(g, device):
            return remote(
                send.at[z, rows_of(g)], x.at[0, z, rows_of(g)], out_send.at[0], row_recv.at[g], device
            )

        def span_of(g, j, way):
            if j < HOPS:
                return rows_of(g)
            return pl.ds(pl.multiple_of(g * cap + way * half, half), half)

        def ring_ref(g, j, way, place):
            return x.at[0, place, span_of(g, j, way)]

        def wait_ring(g, j, way):
            ref = ring_ref(g, j, way, place_of(j, way))
            recv = ring_recv.at[g, way * HOPS + j - 1]
            remote(ref, ref, out_send.at[2], recv, toward_way(way)).wait_recv()

        def send_ring(g, j, way):
            ref = ring_ref(g, j, way, place_of(j - 1, way))
            recv = ring_recv.at[g, way * HOPS + j - 1]
            remote(ref, ref, out_send.at[4 if j < HOPS else 5], recv, toward_way(way)).start()

        def send_twin(g, place, number):
            ref = x.at[0, place, rows_of(g)]
            remote(ref, ref, out_send.at[2], padded_twin.at[number], (c, twin)).start()

        def first(g, b):
            if not isinstance(g, int):
                row_copy(g, (c, lev)).wait_recv()

            for way in range(2):
                send_ring(g, 1, way)
            send_twin(g, z, 5 * b)

        def middle(g, b, j):
            for way in range(2):
                wait_ring(g, j, way)
                send_ring(g, j + 1, way)
                send_twin(g, place_of(j, way), 5 * b + j)

        def last(g, number):
            for way in range(2):
                wait_ring(g, HOPS, way)
            send_twin(g, place_of(HOPS, 0), number)

        def send_rows(b):
            route(z, b, 0)
            for g in range(max(1, b * batch), (b + 1) * batch):
                row_copy(g, (toward(g), lev)).start()

        def group_loop(k, f, steps):
            def body(g):
                f(g)
                for i, step in steps.items():
                    pl.when(g == k * near + i)(step)

            each(k * near, (k + 1) * near, body)

        def enter(k):
            group_loop(k, lambda g: first(g, k // 2), {})

        def turn(k, j, steps):
            group_loop(k, lambda g: middle(g, k // 2, j), steps)

        def leave(k, steps):
            group_loop(k, lambda g: last(g, HOPS if k < 2 else 3 + HOPS + k), steps)

        def own(b, shift, fresh=False):
            return lambda: multiply(b, 0, shift, fresh=fresh)

        def other(b, i):
            def step():
                wait_flat(b * batch + i)
                multiply(b, 1, offset[i])

            return step

        send_rows(0)
        first(0, 0)
        make_pick()
        moved_copy.start()
        each(1, near, lambda g: first(g, 0))
        turn(0, 1, {})
        send_rows(1)
        enter(1)
        turn(0, 2, {})
        wait_weights()
        turn(1, 1, {3: own(0, 0, True)})
        turn(0, 3, {1: own(0, -1), 3: own(0, 1)})
        send_offsets()
        turn(1, 2, {1: other(0, 0)})
        enter(2)
        enter(3)
        leave(0, {})
        turn(1, 3, {1: other(0, 1), 3: other(0, 2)})
        turn(2, 1, {1: own(0, -2), 3: own(0, 2)})
        turn(3, 1, {0: other(0, 3), 2: other(0, 4)})
        leave(1, {0: own(0, -3), 2: own(0, 3)})
        turn(2, 2, {0: other(0, 5), 1: own(0, HOPS), 3: other(0, 6)})
        turn(3, 2, {0: own(1, 0, True), 1: own(1, -1), 2: own(1, 1), 3: other(1, 0)})
        turn(2, 3, {0: other(1, 1), 2: other(1, 2)})
        turn(3, 3, {0: other(0, 7), 1: lambda: finish(0, 0, batch), 2: own(1, -2), 3: own(1, 2)})
        leave(2, {0: other(1, 3), 2: other(1, 4)})
        leave(3, {0: own(1, -3), 1: own(1, 3), 2: other(1, 5), 3: other(1, 6)})
        for s in range(2):
            multiply(1, 0, HOPS, s * near, near)
            wait_flat(15 + s, near)
            multiply(1, 1, HOPS, s * near, near)
            finish(1, s * near, near)

    @pl.when(h == 1)
    def _():
        def number_of(b, i, s):
            return i if b == 0 else batch + i + s

        def flat_ref(p, j, way, place):
            if j < HOPS:
                return flat.at[place, pl.ds(p * piece, piece)]
            return flat.at[place, pl.ds(p * piece + way * (piece // 2), piece // 2)]

        def send_flat(p, j, way):
            ref = flat_ref(p, j, way, place_of(j - 1, way))
            recv = flat_recv.at[p, way * HOPS + j - 1]
            remote(ref, ref, out_send.at[4 if j < HOPS else 5], recv, toward_way(way)).start()

        def hop(j, between=None):
            for p in range(pieces):
                if p == 2 and between is not None:
                    between()
                for way in range(2):
                    ref = flat_ref(p, j, way, place_of(j, way))
                    recv = flat_recv.at[p, way * HOPS + j - 1]
                    remote(ref, ref, out_send.at[4], recv, toward_way(way)).wait_recv()
                    if j < HOPS:
                        send_flat(p, j + 1, way)

        def send_rows(b, i):
            place = place_at(offset[i])
            for g in range(max(1, b * batch), (b + 1) * batch):
                recv = many_recv.at[number_of(b, i, (g - batch) // near if b == 1 and i == RING - 1 else 0)]
                remote(
                    send.at[place, rows_of(g)], x.at[1, place, rows_of(g)], out_send.at[0], recv,
                    (toward(g), lev),
                ).start()

        def arrived(b, i, s=None):
            place = place_at(offset[i])
            start, count = (b * batch, batch) if s is None else (b * batch + s * near, near)
            number = number_of(b, i, s or 0)
            base = max(1, start)
            wait_bytes(
                x.at[1, place, pl.ds(base * cap, (start + count - base) * cap)], many_recv.at[number]
            )
            ref = x.at[1, place, pl.ds(start * cap, count * cap)]
            remote(ref, ref, out_send.at[2], flat_twin.at[number], (c, twin)).start()

        for p in range(pieces):
            for way in range(2):
                send_flat(p, 1, way)
        def pass_on(b, *numbers):
            for i in numbers:
                route(place_at(offset[i]), b, 1)
                send_rows(b, i)

        pass_on(0, 0)
        make_pick()
        moved_copy.start()
        hop(1, lambda: pass_on(1, 0))
        pass_on(0, 1, 2)
        send_offsets()
        arrived(0, 0)
        wait_weights()
        multiply(0, 1, 0, fresh=True)
        hop(2)
        pass_on(0, 3, 4)
        pass_on(1, 1)
        arrived(0, 1)
        arrived(0, 2)
        multiply_two(0, 1, 1)
        hop(3)
        pass_on(0, 5, 6)
        pass_on(1, 2)
        wait_padded(0, 1, 0, batch)
        multiply(0, 0, 0)
        hop(HOPS)
        pass_on(0, 7)
        arrived(0, 3)
        arrived(0, 4)
        pass_on(1, 3, 4)
        multiply_two(0, 1, 2)
        pass_on(1, 5, 6)
        wait_padded(1, 2, 0, batch)
        multiply_two(0, 0, 1)
        pass_on(1, 7)
        arrived(0, 5)
        arrived(0, 6)
        multiply_two(0, 1, 3)
        wait_padded(2, 2, 0, batch)
        multiply_two(0, 0, 2)
        arrived(0, 7)
        arrived(1, 0)
        multiply(0, 1, HOPS)
        wait_padded(3, 2, 0, batch)
        multiply_two(0, 0, 3)
        wait_padded(HOPS, 1, 0, batch)
        multiply(0, 0, HOPS)
        finish(0, 0, batch)
        arrived(1, 1)
        arrived(1, 2)
        multiply(1, 1, 0, fresh=True)
        wait_padded(5, 1, batch, batch)
        multiply(1, 0, 0)
        arrived(1, 3)
        arrived(1, 4)
        multiply_two(1, 1, 1)
        wait_padded(6, 2, batch, batch)
        multiply_two(1, 0, 1)
        arrived(1, 5)
        arrived(1, 6)
        multiply_two(1, 1, 2)
        arrived(1, 7, 0)
        wait_padded(7, 2, batch, batch)
        multiply_two(1, 0, 2)
        arrived(1, 7, 1)
        multiply_two(1, 1, 3)
        wait_padded(8, 2, batch, batch)
        multiply_two(1, 0, 3)
        for s in range(2):
            multiply(1, 1, HOPS, s * near, near)
            wait_padded(5 + HOPS + s, 1, batch + s * near, near)
            multiply(1, 0, HOPS, s * near, near)
            finish(1, s * near, near)

    result[...] = collect(0, batch)
    result[...] += collect(batch, near)
    total = result[...] + collect(batch + near, near)
    sources[...] = total.astype(BF16)

    moved_copy.wait()
    rest = pl.ds(cap, (groups - 1) * cap)

    @pl.when(h == 0)
    def _():
        wait_bytes(send.at[0, rest], out_send.at[0])
        wait_bytes(x.at[0, pl.ds(0, 2 * HOPS - 2)], out_send.at[4])
        wait_bytes(x.at[0, 0], out_send.at[5])

    @pl.when(h == 1)
    def _():
        wait_bytes(send.at[:, rest], out_send.at[0])
        wait_bytes(flat.at[pl.ds(0, 2 * HOPS - 2)], out_send.at[4])
        wait_bytes(flat.at[0], out_send.at[5])

    wait_bytes(off_recv.at[pl.ds(1, groups - 1)], out_send.at[1])
    wait_bytes(x.at[0], out_send.at[2])
    wait_bytes(back_send.at[rest], out_send.at[3])


def shards(
    populations, face_speed, cell_class, class_offset, rate_matrix, slope_matrix, rate_scale, slope_scale
):
    rows, width = populations.shape
    groups = SIDE * SIDE
    cap = 2 * rows // groups
    slots = groups * cap
    vmem = pl.BlockSpec(memory_space=pltpu.VMEM)
    hbm = pl.BlockSpec(memory_space=pl.ANY)
    dma = pltpu.SemaphoreType.DMA
    narrow_sources, transported = pl.pallas_call(
        kernel,
        out_shape=(
            jax.ShapeDtypeStruct((rows, width), BF16), jax.ShapeDtypeStruct((rows, width), F32)
        ),
        in_specs=[hbm] * 8,
        out_specs=(vmem, hbm),
        scratch_shapes=[
            pltpu.VMEM((4, rows // 4), I32),
            pltpu.VMEM(class_offset.shape, BF16),
            pltpu.VMEM(face_speed.shape, F32),
            pltpu.VMEM((1, width), F32),
            pltpu.VMEM((1, width), F32),
            pltpu.VMEM((rows + 16, width), F32),
            pltpu.VMEM((2 * RING, width, width), BF16),
            pltpu.VMEM((2 * RING, width, width), BF16),
            pltpu.VMEM((2, RING, slots, width), BF16),
            pltpu.VMEM((RING, rows, width), BF16),
            pltpu.VMEM((RING, slots, width), BF16),
            pltpu.VMEM((groups // 2, 16, 128), BF16),
            pltpu.VMEM((groups, 16, 128), BF16),
            pltpu.VMEM((slots, width), BF16),
            pltpu.VMEM((slots, width), BF16),
            pltpu.VMEM((slots, rows), BF16),
            pltpu.VMEM((rows, slots), BF16),
            pltpu.VMEM((rows, width), F32),
            pltpu.VMEM((2, slots, width), F32),
            pltpu.VMEM((rows, width), F32),
            dma((8,)),
            dma((2,)),
            dma((2,)),
            dma((6,)),
            dma((groups,)),
            dma((2 * RING + 1,)),
            dma((groups,)),
            dma((groups, RING)),
            dma((4, RING)),
            dma((11,)),
            dma((2 * RING + 1,)),
            dma((groups,)),
        ],
        compiler_params=pltpu.CompilerParams(
            collective_id=0, has_side_effects=True, vmem_limit_bytes=60 * 1024 * 1024
        ),
    )(
        cell_class.reshape(4, -1), class_offset, face_speed,
        populations, rate_matrix, slope_matrix, rate_scale, slope_scale,
    )
    sources = narrow_sources.astype(F32)
    return sources, transported + 0.5 * sources


def solution(mesh):
    in_specs = (
        P("cells", "levels"),
        P(),
        P("cells", None),
        P("cells"),
        P("cells", "levels", None),
        P("cells", "levels", None),
        P("cells", "levels"),
        P("cells", "levels"),
    )
    out_specs = (P("cells", "levels"), P("cells", "levels"))
    return jax.shard_map(shards, mesh=mesh, in_specs=in_specs, out_specs=out_specs, check_vma=False)
```

```python
import jax
import jax.numpy as jnp
from jax import lax
from jax.experimental import pallas as pl
from jax.experimental.pallas import tpu as pltpu
from jax.sharding import PartitionSpec as P

MESH = pl.DeviceIdType.MESH
F32 = jnp.float32
BF16 = jnp.bfloat16
I32 = jnp.int32

SIDE = 4
RING = 8
HOPS = RING // 2


def iota(shape, dim):
    return lax.broadcasted_iota(I32, shape, dim)


def remote(src, dst, send, recv, device):
    return pltpu.make_async_remote_copy(
        src_ref=src, dst_ref=dst, send_sem=send, recv_sem=recv, device_id=device, device_id_type=MESH
    )


def nt(a, b):
    return lax.dot_general(a, b, (((1,), (1,)), ((), ())), preferred_element_type=F32)


def steps_of(g):
    i, j = g // SIDE, g % SIDE
    j = j + (i // 2) * (SIDE - 1 - 2 * j)
    return (i % 2) * 2 + i // 2, j + j // 2 - 2 * (j // 3)


def kernel(
    cls_in, off_in, speeds_in, pop, rate, slope, rate_gain_in, slope_gain_in, sources, transported,
    cls4, off4, speeds, rate_gain, slope_gain, pad, wr, ws, x, flat, send, off_send, off_recv, back_send, back, take, pick, moved, acc, result,
    local_sem, halo_send, halo_recv, out_send, arrive, ring_recv, twin_recv, offs_recv, back_recv,
):
    rows, width = result.shape
    groups = SIDE * SIDE
    cap = back.shape[0] // groups
    batch = groups // 2
    quarter = rows // 4
    c = lax.axis_index("cells")
    lev = lax.axis_index("levels")
    cx, cy = lax.div(c, SIDE), lax.rem(c, SIDE)
    z, h = lax.div(lev, 2), lax.rem(lev, 2)
    right = lax.rem(z + 1, RING) * 2 + h
    left = lax.rem(z + RING - 1, RING) * 2 + h
    twin = z * 2 + 1 - h
    cell_up = lax.rem(c + 1, groups)
    cell_down = lax.rem(c + groups - 1, groups)

    barrier = pltpu.get_barrier_semaphore()

    def toward(g):
        dx, dy = steps_of(g)
        return lax.rem(cx + SIDE - dx, SIDE) * SIDE + lax.rem(cy + SIDE - dy, SIDE)

    def origin(g):
        i, j = lax.div(g, SIDE), lax.rem(g, SIDE)
        j = j + lax.div(i, 2) * (SIDE - 1 - 2 * j)
        dx = lax.rem(i, 2) * 2 + lax.div(i, 2)
        dy = j + lax.div(j, 2) - 2 * lax.div(j, 3)
        return lax.rem(cx + dx, SIDE) * SIDE + lax.rem(cy + dy, SIDE)

    for g in range(1, groups):
        pl.semaphore_signal(barrier, inc=1, device_id=(toward(g), lev), device_id_type=MESH)
    for peer in (right, left, twin):
        pl.semaphore_signal(barrier, inc=1, device_id=(c, peer), device_id_type=MESH)

    pop_copy = pltpu.make_async_copy(pop, pad.at[pl.ds(8, rows)], local_sem.at[0])
    small = [
        pltpu.make_async_copy(src, dst, local_sem.at[3 + i])
        for i, (src, dst) in enumerate((
            (cls_in, cls4), (off_in, off4), (speeds_in, speeds),
            (rate_gain_in, rate_gain), (slope_gain_in, slope_gain),
        ))
    ]
    for copy in small[:3]:
        copy.start()
    pop_copy.start()
    for copy in small[3:]:
        copy.start()
    for i in range(2 * RING):
        lanes = pl.ds(i * width, width)
        pltpu.make_async_copy(rate.at[0, :, lanes], wr.at[i], local_sem.at[1]).start()
        pltpu.make_async_copy(slope.at[0, :, lanes], ws.at[i], local_sem.at[2]).start()

    for copy in small[:3]:
        copy.wait()
    cls = jnp.concatenate([cls4[pl.ds(q, 1), :] for q in range(4)], axis=1)
    hot = (iota((groups, rows), 0) == cls).astype(F32)
    earlier = (iota((rows, rows), 0) < iota((rows, rows), 1)).astype(F32).astype(BF16)
    before = jnp.dot(hot.astype(BF16), earlier, preferred_element_type=F32)
    rank = jnp.sum(hot * before, axis=0, keepdims=True).astype(I32)
    dx = (cx - (cls >> 2)) & (SIDE - 1)
    dy = (cy - (cls & (SIDE - 1))) & (SIDE - 1)
    i, j = (dx & 1) * 2 + (dx >> 1), dy ^ (dy >> 1)
    j = j + (i >> 1) * (SIDE - 1 - 2 * j)
    slot = (i * SIDE + j) * cap + rank

    slot4 = jnp.concatenate([slot[:, q * quarter : (q + 1) * quarter] for q in range(4)], axis=0)
    base = pl.multiple_of(c * rows, rows)
    line = [speeds[pl.ds(base + q * quarter, quarter)].reshape(1, quarter) for q in range(4)]
    end = speeds[pl.ds(base + rows, 1)].reshape(1, 1)
    line = jnp.concatenate(line + [jnp.broadcast_to(end, (1, quarter))], axis=1)
    ahead = pltpu.roll(line, 5 * quarter - 1, 1)
    o4 = off4[...].astype(F32).reshape(4, quarter)
    columns = jnp.concatenate(
        [line[:, q * quarter : (q + 1) * quarter] for q in range(4)] +
        [ahead[:, q * quarter : (q + 1) * quarter] for q in range(4)] +
        [slot4.astype(F32), jnp.zeros((116, 128), F32)], axis=0
    ).T

    def column(i):
        return columns[:, i : i + 1]

    pop_copy.wait()
    pl.semaphore_wait(barrier, groups - 1 + 3)

    up = remote(
        pad.at[pl.ds(rows, 8)], pad.at[pl.ds(0, 8)], halo_send.at[0], halo_recv.at[0], (cell_up, lev)
    )
    down = remote(
        pad.at[pl.ds(8, 8)], pad.at[pl.ds(rows + 8, 8)], halo_send.at[1], halo_recv.at[1], (cell_down, lev)
    )
    up.start()
    down.start()

    for q in range(4):
        take[pl.ds(4 * cap * q, 4 * cap), :] = (
            (iota((4 * cap, rows), 0) + 4 * cap * q == slot).astype(F32).astype(BF16)
        )

    def transport(start, count):
        q, r = start // quarter, start % quarter
        a = pad[pl.ds(start + 7, count), :]
        b = pad[pl.ds(start + 8, count), :]
        d = pad[pl.ds(start + 9, count), :]
        lower = 0.5 * column(q)[r : r + count] * (a + b) - 0.625 * (b - a)
        upper = 0.5 * column(4 + q)[r : r + count] * (b + d) - 0.625 * (d - b)
        t = b + 0.4 * (lower - upper)
        moved[pl.ds(start, count), :] = t
        flat[z, pl.ds(start, count), :] = t.astype(BF16)

    edge = 16
    transport(edge, quarter - edge)
    transport(quarter, quarter)
    transport(2 * quarter, quarter)
    transport(3 * quarter, quarter - edge)
    up.wait()
    down.wait()

    @pl.when(c == 0)
    def _():
        pad[pl.ds(0, 8), :] = jnp.zeros((8, width), F32)

    @pl.when(c == groups - 1)
    def _():
        pad[pl.ds(rows + 8, 8), :] = jnp.zeros((8, width), F32)

    transport(0, edge)
    transport(rows - edge, edge)

    offsets = jnp.broadcast_to(
        jnp.concatenate([o4[q : q + 1] for q in range(4)], axis=1), (16, rows)
    ).astype(BF16)
    moved_copy = pltpu.make_async_copy(moved, transported, local_sem.at[0])

    half = cap // 2
    near = batch // 2
    pieces = 4
    piece = rows // pieces
    offset = (0, -1, 1, -2, 2, -3, 3, HOPS)

    def rows_of(g):
        return pl.ds(pl.multiple_of(g * cap, cap), cap)

    def place_at(i):
        return lax.rem(z + RING + i, RING)

    def place_of(j, way):
        return place_at(-j if way == 0 else j)

    def toward_way(way):
        return (c, right if way == 0 else left)

    def each(lower, upper, f):
        def body(g, carry):
            f(g)
            return carry

        lax.fori_loop(lower, upper, body, 0)

    def route(place, b, own_role):
        for q in range(2):
            span = pl.ds((b * batch + q * near) * cap, near * cap)
            got = jnp.dot(take[span, :], flat[place], preferred_element_type=F32).astype(BF16)
            send[place, span, :] = got
            if b == 0 and q == 0:
                x[own_role, place, pl.ds(0, cap), :] = got[:cap]

    def part_of(g):
        return max(0, g // near - 1)

    def off_copy(g, device):
        return remote(off_send.at[g // 2], off_recv.at[g], out_send.at[1], offs_recv.at[part_of(g)], device)

    def send_offsets():
        got = nt(offsets, take[...]).astype(BF16)
        for p in range(batch):
            off_send[p] = got[:, 2 * cap * p : 2 * cap * (p + 1)]
        off_recv[0] = got[:, : 2 * cap]
        for g in range(1, groups):
            off_copy(g, (toward(g), lev)).start()

    def make_pick():
        for q in range(4):
            pick[pl.ds(q * quarter, quarter), :] = (
                (iota((quarter, groups * cap), 1) == column(8 + q).astype(I32)).astype(F32).astype(BF16)
            )

    def wait_bytes(ref, sem):
        pltpu.make_async_copy(ref, ref, sem).wait()

    def wait_weights():
        wait_bytes(wr, local_sem.at[1])
        wait_bytes(ws, local_sem.at[2])
        for copy in small[3:]:
            copy.wait()

    def multiply(b, role, shift, start=0, count=batch, fresh=False):
        place = place_at(shift)
        level = place * 2 + role
        span = pl.ds((b * batch + start) * cap, count * cap)
        chunk = x[role, place, span, :]
        for n, w in ((0, wr), (1, ws)):
            part = nt(chunk, w[level])
            acc[n, span, :] = part if fresh else acc[n, span, :] + part

    def multiply_two(b, role, j):
        each(0, 2, lambda i: multiply(b, role, j * (2 * i - 1)))

    def when(i, at, f):
        pl.when(i == at)(f)

    def back_copy(g, device):
        return remote(
            back_send.at[rows_of(g)], back.at[rows_of(g)], out_send.at[3], back_recv.at[part_of(g)], device
        )

    def finish(b, start, count):
        base = b * batch + start
        start = max(1, base)
        wait_bytes(off_recv.at[pl.ds(start, base + count - start)], offs_recv.at[part_of(base)])
        low = iota((1, 2 * cap), 1) < cap
        o = [
            jnp.where(low, off_recv[g, 0:1, :].astype(F32), off_recv[g + 1, 0:1, :].astype(F32))
            for g in range(base, base + count, 2)
        ]
        o = jnp.concatenate(o + [jnp.zeros((128 - len(o), 2 * cap), F32)], axis=0).T
        for p in range(count // 2):
            two = pl.ds((base + 2 * p) * cap, 2 * cap)
            values = rate_gain[...] * acc[0, two, :] + slope_gain[...] * o[:, p : p + 1] * acc[1, two, :]
            back_send[two, :] = values.astype(BF16)
            if base + p == 0:
                back[pl.ds(0, cap), :] = values[:cap].astype(BF16)
        for g in range(max(1, base), base + count):
            back_copy(g, (origin(g), lev)).start()

    def collect(base, count):
        start = max(1, base)
        wait_bytes(back.at[pl.ds(start * cap, (base + count - start) * cap)], back_recv.at[part_of(base)])
        span = pl.ds(base * cap, count * cap)
        return jnp.dot(pick[:, span], back[span, :], preferred_element_type=F32)

    def wait_padded(number, chunks, start, count):
        wait_bytes(x.at[0, pl.ds(0, chunks), pl.ds(start * cap, count * cap)], twin_recv.at[number])

    def wait_flat(number, count=batch):
        wait_bytes(x.at[1, 0, pl.ds(0, count * cap)], twin_recv.at[number])

    @pl.when(h == 0)
    def _():
        def row_copy(g, device):
            return remote(
                send.at[z, rows_of(g)], x.at[0, z, rows_of(g)], out_send.at[0], arrive.at[g], device
            )

        def span_of(g, j, way):
            if j < HOPS:
                return rows_of(g)
            return pl.ds(pl.multiple_of(g * cap + way * half, half), half)

        def ring_ref(g, j, way, place):
            return x.at[0, place, span_of(g, j, way)]

        def wait_ring(g, j):
            ref = x.at[0, pl.ds(0, 2), rows_of(g)] if j < HOPS else x.at[0, 0, rows_of(g)]
            wait_bytes(ref, ring_recv.at[g, j - 1])

        def send_ring(g, j, way):
            ref = ring_ref(g, j, way, place_of(j - 1, way))
            remote(
                ref, ref, out_send.at[4 if j < HOPS else 5], ring_recv.at[g, j - 1], toward_way(way)
            ).start()

        def send_twin(g, place, number):
            ref = x.at[0, place, rows_of(g)]
            remote(ref, ref, out_send.at[2], twin_recv.at[number], (c, twin)).start()

        def first(g, b):
            if not isinstance(g, int):
                row_copy(g, (c, lev)).wait_recv()

            for way in range(2):
                send_ring(g, 1, way)
            send_twin(g, z, 5 * b)

        def middle(g, b, j):
            wait_ring(g, j)
            for way in range(2):
                send_ring(g, j + 1, way)
                send_twin(g, place_of(j, way), 5 * b + j)

        def last(g, number):
            wait_ring(g, HOPS)
            send_twin(g, place_of(HOPS, 0), number)

        def send_rows(b):
            route(z, b, 0)
            for g in range(max(1, b * batch), (b + 1) * batch):
                row_copy(g, (toward(g), lev)).start()

        def group_loop(k, f, steps):
            def body(g):
                f(g)
                for i, step in steps.items():
                    pl.when(g == k * near + i)(step)

            each(k * near, (k + 1) * near, body)

        def enter(k):
            group_loop(k, lambda g: first(g, k // 2), {})

        def turn(k, j, steps):
            group_loop(k, lambda g: middle(g, k // 2, j), steps)

        def leave(k, steps):
            group_loop(k, lambda g: last(g, HOPS if k < 2 else 3 + HOPS + k), steps)

        def own(b, shift, fresh=False):
            return lambda: multiply(b, 0, shift, fresh=fresh)

        def other(b, i):
            def step():
                wait_flat(b * batch + i)
                multiply(b, 1, offset[i])

            return step

        send_rows(0)
        first(0, 0)
        make_pick()
        moved_copy.start()
        each(1, near, lambda g: first(g, 0))
        turn(0, 1, {})
        send_rows(1)
        enter(1)
        turn(0, 2, {})
        wait_weights()
        turn(1, 1, {3: own(0, 0, True)})
        turn(0, 3, {1: own(0, -1), 3: own(0, 1)})
        send_offsets()
        turn(1, 2, {1: other(0, 0)})
        enter(2)
        enter(3)
        leave(0, {})
        turn(1, 3, {1: other(0, 1), 3: other(0, 2)})
        turn(2, 1, {1: own(0, -2), 3: own(0, 2)})
        turn(3, 1, {0: other(0, 3), 2: other(0, 4)})
        leave(1, {0: own(0, -3), 2: own(0, 3)})
        turn(2, 2, {0: other(0, 5), 1: own(0, HOPS), 3: other(0, 6)})
        turn(3, 2, {0: own(1, 0, True), 1: own(1, -1), 2: own(1, 1), 3: other(1, 0)})
        turn(2, 3, {0: other(1, 1), 2: other(1, 2)})
        turn(3, 3, {0: other(0, 7), 1: lambda: finish(0, 0, batch), 2: own(1, -2), 3: own(1, 2)})
        leave(2, {0: other(1, 3), 2: other(1, 4)})
        def half_own(s):
            multiply(1, 0, -3, s * near, near)
            multiply(1, 0, 3, s * near, near)

        def half_other(s):
            if s == 0:
                wait_flat(batch + 5)
                wait_flat(batch + 6)
            multiply(1, 1, -3, s * near, near)
            multiply(1, 1, 3, s * near, near)

        def half_end(s):
            multiply(1, 0, HOPS, s * near, near)
            wait_flat(15 + s, near)
            multiply(1, 1, HOPS, s * near, near)
            finish(1, s * near, near)

        leave(3, {
            0: lambda: half_own(0), 1: lambda: half_other(0), 2: lambda: half_end(0), 3: lambda: half_own(1)
        })
        half_other(1)
        half_end(1)

    @pl.when(h == 1)
    def _():
        def number_of(b, i, s):
            return i if b == 0 else batch + i + s

        def flat_ref(p, j, way, place):
            if j < HOPS:
                return flat.at[place, pl.ds(p * piece, piece)]
            return flat.at[place, pl.ds(p * piece + way * (piece // 2), piece // 2)]

        def send_flat(p, j, way):
            ref = flat_ref(p, j, way, place_of(j - 1, way))
            remote(
                ref, ref, out_send.at[4 if j < HOPS else 5], ring_recv.at[p, j - 1], toward_way(way)
            ).start()

        def hop(j, between=None):
            for p in range(pieces):
                if p == 2 and between is not None:
                    between()
                span = pl.ds(p * piece, piece)
                ref = flat.at[pl.ds(0, 2), span] if j < HOPS else flat.at[0, span]
                wait_bytes(ref, ring_recv.at[p, j - 1])
                if j < HOPS:
                    for way in range(2):
                        send_flat(p, j + 1, way)

        def send_rows(b, i):
            place = place_at(offset[i])
            for g in range(max(1, b * batch), (b + 1) * batch):
                recv = arrive.at[number_of(b, i, (g - batch) // near if b == 1 and i == RING - 1 else 0)]
                remote(
                    send.at[place, rows_of(g)], x.at[1, place, rows_of(g)], out_send.at[0], recv,
                    (toward(g), lev),
                ).start()

        def arrived(b, i, s=None):
            place = place_at(offset[i])
            start, count = (b * batch, batch) if s is None else (b * batch + s * near, near)
            number = number_of(b, i, s or 0)
            base = max(1, start)
            wait_bytes(
                x.at[1, place, pl.ds(base * cap, (start + count - base) * cap)], arrive.at[number]
            )
            ref = x.at[1, place, pl.ds(start * cap, count * cap)]
            remote(ref, ref, out_send.at[2], twin_recv.at[number], (c, twin)).start()

        for p in range(pieces):
            for way in range(2):
                send_flat(p, 1, way)
        def pass_on(b, *numbers):
            for i in numbers:
                route(place_at(offset[i]), b, 1)
                send_rows(b, i)

        pass_on(0, 0)
        make_pick()
        moved_copy.start()
        hop(1, lambda: pass_on(1, 0))
        pass_on(0, 1, 2)
        send_offsets()
        arrived(0, 0)
        wait_weights()
        multiply(0, 1, 0, fresh=True)
        hop(2)
        pass_on(0, 3, 4)
        pass_on(1, 1)
        arrived(0, 1)
        arrived(0, 2)
        multiply_two(0, 1, 1)
        hop(3)
        pass_on(0, 5, 6)
        pass_on(1, 2)
        wait_padded(0, 1, 0, batch)
        multiply(0, 0, 0)
        hop(HOPS)
        pass_on(0, 7)
        arrived(0, 3)
        arrived(0, 4)
        pass_on(1, 3, 4)
        multiply_two(0, 1, 2)
        pass_on(1, 5, 6)
        wait_padded(1, 2, 0, batch)
        multiply_two(0, 0, 1)
        pass_on(1, 7)
        arrived(0, 5)
        arrived(0, 6)
        arrived(1, 0)
        multiply_two(0, 1, 3)
        wait_padded(2, 2, 0, batch)
        multiply_two(0, 0, 2)
        arrived(1, 1)
        arrived(1, 2)
        wait_padded(3, 2, 0, batch)
        multiply_two(0, 0, 3)
        arrived(0, 7)
        multiply(0, 1, HOPS)
        wait_padded(HOPS, 1, 0, batch)
        multiply(0, 0, HOPS)
        finish(0, 0, batch)
        multiply(1, 1, 0, fresh=True)
        wait_padded(5, 1, batch, batch)
        multiply(1, 0, 0)
        arrived(1, 3)
        arrived(1, 4)
        multiply_two(1, 1, 1)
        wait_padded(6, 2, batch, batch)
        multiply_two(1, 0, 1)
        arrived(1, 5)
        arrived(1, 6)
        multiply_two(1, 1, 2)
        arrived(1, 7, 0)
        wait_padded(7, 2, batch, batch)
        multiply_two(1, 0, 2)
        arrived(1, 7, 1)
        multiply_two(1, 1, 3)
        wait_padded(8, 2, batch, batch)
        multiply_two(1, 0, 3)
        for s in range(2):
            multiply(1, 1, HOPS, s * near, near)
            wait_padded(5 + HOPS + s, 1, batch + s * near, near)
            multiply(1, 0, HOPS, s * near, near)
            finish(1, s * near, near)

    result[...] = collect(0, batch)
    result[...] += collect(batch, near)
    total = result[...] + collect(batch + near, near)
    sources[...] = total.astype(BF16)

    moved_copy.wait()
    rest = pl.ds(cap, (groups - 1) * cap)

    @pl.when(h == 0)
    def _():
        wait_bytes(send.at[0, rest], out_send.at[0])
        wait_bytes(x.at[0, pl.ds(0, 2 * HOPS - 2)], out_send.at[4])
        wait_bytes(x.at[0, 0], out_send.at[5])

    @pl.when(h == 1)
    def _():
        wait_bytes(send.at[:, rest], out_send.at[0])
        wait_bytes(flat.at[pl.ds(0, 2 * HOPS - 2)], out_send.at[4])
        wait_bytes(flat.at[0], out_send.at[5])

    wait_bytes(off_recv.at[pl.ds(1, groups - 1)], out_send.at[1])
    wait_bytes(x.at[0], out_send.at[2])
    wait_bytes(back_send.at[rest], out_send.at[3])


def shards(
    populations, face_speed, cell_class, class_offset, rate_matrix, slope_matrix, rate_scale, slope_scale
):
    rows, width = populations.shape
    groups = SIDE * SIDE
    cap = 2 * rows // groups
    slots = groups * cap
    vmem = pl.BlockSpec(memory_space=pltpu.VMEM)
    hbm = pl.BlockSpec(memory_space=pl.ANY)
    dma = pltpu.SemaphoreType.DMA
    narrow_sources, transported = pl.pallas_call(
        kernel,
        out_shape=(
            jax.ShapeDtypeStruct((rows, width), BF16), jax.ShapeDtypeStruct((rows, width), F32)
        ),
        in_specs=[hbm] * 8,
        out_specs=(vmem, hbm),
        scratch_shapes=[
            pltpu.VMEM((4, rows // 4), I32),
            pltpu.VMEM(class_offset.shape, BF16),
            pltpu.VMEM(face_speed.shape, F32),
            pltpu.VMEM((1, width), F32),
            pltpu.VMEM((1, width), F32),
            pltpu.VMEM((rows + 16, width), F32),
            pltpu.VMEM((2 * RING, width, width), BF16),
            pltpu.VMEM((2 * RING, width, width), BF16),
            pltpu.VMEM((2, RING, slots, width), BF16),
            pltpu.VMEM((RING, rows, width), BF16),
            pltpu.VMEM((RING, slots, width), BF16),
            pltpu.VMEM((groups // 2, 16, 128), BF16),
            pltpu.VMEM((groups, 16, 128), BF16),
            pltpu.VMEM((slots, width), BF16),
            pltpu.VMEM((slots, width), BF16),
            pltpu.VMEM((slots, rows), BF16),
            pltpu.VMEM((rows, slots), BF16),
            pltpu.VMEM((rows, width), F32),
            pltpu.VMEM((2, slots, width), F32),
            pltpu.VMEM((rows, width), F32),
            dma((8,)),
            dma((2,)),
            dma((2,)),
            dma((6,)),
            dma((2 * RING + 1,)),
            dma((groups, HOPS)),
            dma((2 * RING + 1,)),
            dma((3,)),
            dma((3,)),
        ],
        compiler_params=pltpu.CompilerParams(
            collective_id=0, has_side_effects=True, vmem_limit_bytes=60 * 1024 * 1024
        ),
    )(
        cell_class.reshape(4, -1), class_offset, face_speed,
        populations, rate_matrix, slope_matrix, rate_scale, slope_scale,
    )
    sources = narrow_sources.astype(F32)
    return sources, transported + 0.5 * sources


def solution(mesh):
    in_specs = (
        P("cells", "levels"),
        P(),
        P("cells", None),
        P("cells"),
        P("cells", "levels", None),
        P("cells", "levels", None),
        P("cells", "levels"),
        P("cells", "levels"),
    )
    out_specs = (P("cells", "levels"), P("cells", "levels"))
    return jax.shard_map(shards, mesh=mesh, in_specs=in_specs, out_specs=out_specs, check_vma=False)
```

```python
import jax
import jax.numpy as jnp
from jax import lax
from jax.experimental import pallas as pl
from jax.experimental.pallas import tpu as pltpu
from jax.sharding import PartitionSpec as P

MESH = pl.DeviceIdType.MESH
F32 = jnp.float32
BF16 = jnp.bfloat16
I32 = jnp.int32

SIDE = 4
RING = 8
HOPS = RING // 2


def iota(shape, dim):
    return lax.broadcasted_iota(I32, shape, dim)


def remote(src, dst, send, recv, device):
    return pltpu.make_async_remote_copy(
        src_ref=src, dst_ref=dst, send_sem=send, recv_sem=recv, device_id=device, device_id_type=MESH
    )


def nt(a, b):
    return lax.dot_general(a, b, (((1,), (1,)), ((), ())), preferred_element_type=F32)


def steps_of(g):
    i, j = g // SIDE, g % SIDE
    j = j + (i // 2) * (SIDE - 1 - 2 * j)
    return (i % 2) * 2 + i // 2, j + j // 2 - 2 * (j // 3)


def kernel(
    cls_in, off_in, speeds_in, pop, rate, slope, rate_gain_in, slope_gain_in, sources, transported,
    cls4, off4, speeds, rate_gain, slope_gain, pad, wr, ws, x, flat, send, off_send, off_recv, back_send, back, take, pick, moved, acc, result,
    local_sem, halo_send, halo_recv, out_send, arrive, ring_recv, twin_recv, offs_recv, back_recv,
):
    rows, width = result.shape
    groups = SIDE * SIDE
    cap = back.shape[0] // groups
    batch = groups // 2
    quarter = rows // 4
    c = lax.axis_index("cells")
    lev = lax.axis_index("levels")
    cx, cy = lax.div(c, SIDE), lax.rem(c, SIDE)
    z, h = lax.div(lev, 2), lax.rem(lev, 2)
    right = lax.rem(z + 1, RING) * 2 + h
    left = lax.rem(z + RING - 1, RING) * 2 + h
    twin = z * 2 + 1 - h
    cell_up = lax.rem(c + 1, groups)
    cell_down = lax.rem(c + groups - 1, groups)

    barrier = pltpu.get_barrier_semaphore()

    def toward(g):
        dx, dy = steps_of(g)
        return lax.rem(cx + SIDE - dx, SIDE) * SIDE + lax.rem(cy + SIDE - dy, SIDE)

    def origin(g):
        i, j = lax.div(g, SIDE), lax.rem(g, SIDE)
        j = j + lax.div(i, 2) * (SIDE - 1 - 2 * j)
        dx = lax.rem(i, 2) * 2 + lax.div(i, 2)
        dy = j + lax.div(j, 2) - 2 * lax.div(j, 3)
        return lax.rem(cx + dx, SIDE) * SIDE + lax.rem(cy + dy, SIDE)

    for g in range(1, groups):
        pl.semaphore_signal(barrier, inc=1, device_id=(toward(g), lev), device_id_type=MESH)
    for peer in (right, left, twin):
        pl.semaphore_signal(barrier, inc=1, device_id=(c, peer), device_id_type=MESH)

    pop_copy = pltpu.make_async_copy(pop, pad.at[pl.ds(8, rows)], local_sem.at[0])
    small = [
        pltpu.make_async_copy(src, dst, local_sem.at[3 + i])
        for i, (src, dst) in enumerate((
            (cls_in, cls4), (off_in, off4), (speeds_in, speeds),
            (rate_gain_in, rate_gain), (slope_gain_in, slope_gain),
        ))
    ]
    for copy in small[:3]:
        copy.start()
    pop_copy.start()
    for copy in small[3:]:
        copy.start()
    for i in range(2 * RING):
        lanes = pl.ds(i * width, width)
        pltpu.make_async_copy(rate.at[0, :, lanes], wr.at[i], local_sem.at[1]).start()
        pltpu.make_async_copy(slope.at[0, :, lanes], ws.at[i], local_sem.at[2]).start()

    for copy in small[:3]:
        copy.wait()
    cls = jnp.concatenate([cls4[pl.ds(q, 1), :] for q in range(4)], axis=1)
    hot = (iota((groups, rows), 0) == cls).astype(F32)
    earlier = (iota((rows, rows), 0) < iota((rows, rows), 1)).astype(F32).astype(BF16)
    before = jnp.dot(hot.astype(BF16), earlier, preferred_element_type=F32)
    rank = jnp.sum(hot * before, axis=0, keepdims=True).astype(I32)
    dx = (cx - (cls >> 2)) & (SIDE - 1)
    dy = (cy - (cls & (SIDE - 1))) & (SIDE - 1)
    i, j = (dx & 1) * 2 + (dx >> 1), dy ^ (dy >> 1)
    j = j + (i >> 1) * (SIDE - 1 - 2 * j)
    slot = (i * SIDE + j) * cap + rank

    slot4 = jnp.concatenate([slot[:, q * quarter : (q + 1) * quarter] for q in range(4)], axis=0)
    base = pl.multiple_of(c * rows, rows)
    line = [speeds[pl.ds(base + q * quarter, quarter)].reshape(1, quarter) for q in range(4)]
    end = speeds[pl.ds(base + rows, 1)].reshape(1, 1)
    line = jnp.concatenate(line + [jnp.broadcast_to(end, (1, quarter))], axis=1)
    ahead = pltpu.roll(line, 5 * quarter - 1, 1)
    o4 = off4[...].astype(F32).reshape(4, quarter)
    columns = jnp.concatenate(
        [line[:, q * quarter : (q + 1) * quarter] for q in range(4)] +
        [ahead[:, q * quarter : (q + 1) * quarter] for q in range(4)] +
        [slot4.astype(F32), jnp.zeros((116, 128), F32)], axis=0
    ).T

    def column(i):
        return columns[:, i : i + 1]

    pop_copy.wait()
    pl.semaphore_wait(barrier, groups - 1 + 3)

    up = remote(
        pad.at[pl.ds(rows, 8)], pad.at[pl.ds(0, 8)], halo_send.at[0], halo_recv.at[0], (cell_up, lev)
    )
    down = remote(
        pad.at[pl.ds(8, 8)], pad.at[pl.ds(rows + 8, 8)], halo_send.at[1], halo_recv.at[1], (cell_down, lev)
    )
    up.start()
    down.start()

    for q in range(4):
        take[pl.ds(4 * cap * q, 4 * cap), :] = (
            (iota((4 * cap, rows), 0) + 4 * cap * q == slot).astype(F32).astype(BF16)
        )

    def transport(start, count):
        q, r = start // quarter, start % quarter
        a = pad[pl.ds(start + 7, count), :]
        b = pad[pl.ds(start + 8, count), :]
        d = pad[pl.ds(start + 9, count), :]
        lower = 0.5 * column(q)[r : r + count] * (a + b) - 0.625 * (b - a)
        upper = 0.5 * column(4 + q)[r : r + count] * (b + d) - 0.625 * (d - b)
        t = b + 0.4 * (lower - upper)
        moved[pl.ds(start, count), :] = t
        flat[z, pl.ds(start, count), :] = t.astype(BF16)

    edge = 16
    transport(edge, quarter - edge)
    transport(quarter, quarter)
    transport(2 * quarter, quarter)
    transport(3 * quarter, quarter - edge)
    up.wait()
    down.wait()

    @pl.when(c == 0)
    def _():
        pad[pl.ds(0, 8), :] = jnp.zeros((8, width), F32)

    @pl.when(c == groups - 1)
    def _():
        pad[pl.ds(rows + 8, 8), :] = jnp.zeros((8, width), F32)

    transport(0, edge)
    transport(rows - edge, edge)

    offsets = jnp.broadcast_to(
        jnp.concatenate([o4[q : q + 1] for q in range(4)], axis=1), (16, rows)
    ).astype(BF16)
    moved_copy = pltpu.make_async_copy(moved, transported, local_sem.at[0])

    half = cap // 2
    near = batch // 2
    pieces = 4
    piece = rows // pieces
    offset = (0, -1, 1, -2, 2, -3, 3, HOPS)

    def rows_of(g):
        return pl.ds(pl.multiple_of(g * cap, cap), cap)

    def place_at(i):
        return lax.rem(z + RING + i, RING)

    def place_of(j, way):
        return place_at(-j if way == 0 else j)

    def toward_way(way):
        return (c, right if way == 0 else left)

    def each(lower, upper, f):
        def body(g, carry):
            f(g)
            return carry

        lax.fori_loop(lower, upper, body, 0)

    def route(place, b, own_role):
        for q in range(2):
            span = pl.ds((b * batch + q * near) * cap, near * cap)
            got = jnp.dot(take[span, :], flat[place], preferred_element_type=F32).astype(BF16)
            send[place, span, :] = got
            if b == 0 and q == 0:
                x[own_role, place, pl.ds(0, cap), :] = got[:cap]

    def part_of(g):
        return max(0, g // near - 1)

    def off_copy(g, device):
        return remote(off_send.at[g // 2], off_recv.at[g], out_send.at[1], offs_recv.at[part_of(g)], device)

    def send_offsets():
        got = nt(offsets, take[...]).astype(BF16)
        for p in range(batch):
            off_send[p] = got[:, 2 * cap * p : 2 * cap * (p + 1)]
        off_recv[0] = got[:, : 2 * cap]
        for g in range(1, groups):
            off_copy(g, (toward(g), lev)).start()

    def make_pick():
        for q in range(4):
            pick[pl.ds(q * quarter, quarter), :] = (
                (iota((quarter, groups * cap), 1) == column(8 + q).astype(I32)).astype(F32).astype(BF16)
            )

    def wait_bytes(ref, sem):
        pltpu.make_async_copy(ref, ref, sem).wait()

    def wait_weights():
        wait_bytes(wr, local_sem.at[1])
        wait_bytes(ws, local_sem.at[2])
        for copy in small[3:]:
            copy.wait()

    def multiply(b, role, shift, start=0, count=batch, fresh=False):
        place = place_at(shift)
        level = place * 2 + role
        span = pl.ds((b * batch + start) * cap, count * cap)
        chunk = x[role, place, span, :]
        for n, w in ((0, wr), (1, ws)):
            part = nt(chunk, w[level])
            acc[n, span, :] = part if fresh else acc[n, span, :] + part

    def multiply_two(b, role, j):
        each(0, 2, lambda i: multiply(b, role, j * (2 * i - 1)))

    def when(i, at, f):
        pl.when(i == at)(f)

    def back_copy(g, device):
        return remote(
            back_send.at[rows_of(g)], back.at[rows_of(g)], out_send.at[3], back_recv.at[part_of(g)], device
        )

    def finish(b, start, count):
        base = b * batch + start
        start = max(1, base)
        wait_bytes(off_recv.at[pl.ds(start, base + count - start)], offs_recv.at[part_of(base)])
        low = iota((1, 2 * cap), 1) < cap
        o = [
            jnp.where(low, off_recv[g, 0:1, :].astype(F32), off_recv[g + 1, 0:1, :].astype(F32))
            for g in range(base, base + count, 2)
        ]
        o = jnp.concatenate(o + [jnp.zeros((128 - len(o), 2 * cap), F32)], axis=0).T
        for p in range(count // 2):
            two = pl.ds((base + 2 * p) * cap, 2 * cap)
            values = rate_gain[...] * acc[0, two, :] + slope_gain[...] * o[:, p : p + 1] * acc[1, two, :]
            back_send[two, :] = values.astype(BF16)
            if base + p == 0:
                back[pl.ds(0, cap), :] = values[:cap].astype(BF16)
        for g in range(max(1, base), base + count):
            back_copy(g, (origin(g), lev)).start()

    def collect(base, count):
        start = max(1, base)
        wait_bytes(back.at[pl.ds(start * cap, (base + count - start) * cap)], back_recv.at[part_of(base)])
        span = pl.ds(base * cap, count * cap)
        return jnp.dot(pick[:, span], back[span, :], preferred_element_type=F32)

    def wait_padded(number, chunks, start, count):
        wait_bytes(x.at[0, pl.ds(0, chunks), pl.ds(start * cap, count * cap)], twin_recv.at[number])

    def wait_flat(number, count=batch):
        wait_bytes(x.at[1, 0, pl.ds(0, count * cap)], twin_recv.at[number])

    @pl.when(h == 0)
    def _():
        def row_copy(g, device):
            return remote(
                send.at[z, rows_of(g)], x.at[0, z, rows_of(g)], out_send.at[0], arrive.at[g], device
            )

        def span_of(g, j, way):
            if j < HOPS:
                return rows_of(g)
            return pl.ds(pl.multiple_of(g * cap + way * half, half), half)

        def ring_ref(g, j, way, place):
            return x.at[0, place, span_of(g, j, way)]

        def wait_ring(g, j):
            ref = x.at[0, pl.ds(0, 2), rows_of(g)] if j < HOPS else x.at[0, 0, rows_of(g)]
            wait_bytes(ref, ring_recv.at[g, j - 1])

        def send_ring(g, j, way):
            ref = ring_ref(g, j, way, place_of(j - 1, way))
            remote(
                ref, ref, out_send.at[4 if j < HOPS else 5], ring_recv.at[g, j - 1], toward_way(way)
            ).start()

        def send_twin(g, place, number):
            ref = x.at[0, place, rows_of(g)]
            remote(ref, ref, out_send.at[2], twin_recv.at[number], (c, twin)).start()

        def first(g, b):
            if not isinstance(g, int):
                row_copy(g, (c, lev)).wait_recv()

            for way in range(2):
                send_ring(g, 1, way)
            send_twin(g, z, 5 * b)

        def middle(g, b, j):
            wait_ring(g, j)
            for way in range(2):
                send_ring(g, j + 1, way)
                send_twin(g, place_of(j, way), 5 * b + j)

        def last(g, number):
            wait_ring(g, HOPS)
            send_twin(g, place_of(HOPS, 0), number)

        def send_rows(b):
            route(z, b, 0)
            for g in range(max(1, b * batch), (b + 1) * batch):
                row_copy(g, (toward(g), lev)).start()

        def group_loop(k, f, steps):
            def body(g):
                f(g)
                for i, step in steps.items():
                    pl.when(g == k * near + i)(step)

            each(k * near, (k + 1) * near, body)

        def enter(k):
            group_loop(k, lambda g: first(g, k // 2), {})

        def turn(k, j, steps):
            group_loop(k, lambda g: middle(g, k // 2, j), steps)

        def leave(k, steps):
            group_loop(k, lambda g: last(g, HOPS if k < 2 else 3 + HOPS + k), steps)

        def own(b, shift, fresh=False):
            return lambda: multiply(b, 0, shift, fresh=fresh)

        def other(b, i):
            def step():
                wait_flat(b * batch + i)
                multiply(b, 1, offset[i])

            return step

        send_rows(0)
        first(0, 0)
        make_pick()
        moved_copy.start()
        each(1, near, lambda g: first(g, 0))
        turn(0, 1, {})
        send_rows(1)
        enter(1)
        turn(0, 2, {})
        wait_weights()
        turn(1, 1, {0: own(0, 0, True), 2: other(0, 0)})
        turn(0, 3, {0: other(0, 1), 2: other(0, 2)})
        send_offsets()
        turn(1, 2, {1: own(0, -1), 3: own(0, 1)})
        enter(2)
        enter(3)
        leave(0, {1: own(0, -2), 3: own(0, 2)})
        turn(1, 3, {1: other(0, 3), 3: other(0, 4)})
        turn(2, 1, {1: own(0, -3), 3: own(0, 3)})
        turn(3, 1, {1: other(0, 5)})
        leave(1, {})
        turn(2, 2, {0: own(0, HOPS), 2: own(1, 0, True)})
        turn(3, 2, {0: own(1, -1), 2: own(1, 1), 3: other(1, 0)})
        turn(2, 3, {0: other(1, 1), 2: other(1, 2)})
        turn(3, 3, {0: other(0, 6), 1: other(0, 7), 2: lambda: finish(0, 0, batch), 3: own(1, -2)})
        leave(2, {0: own(1, 2), 1: other(1, 3), 2: other(1, 4)})

        def half_own(s):
            multiply(1, 0, -3, s * near, near)
            multiply(1, 0, 3, s * near, near)

        def half_other(s):
            if s == 0:
                wait_flat(batch + 5)
                wait_flat(batch + 6)
            multiply(1, 1, -3, s * near, near)
            multiply(1, 1, 3, s * near, near)

        def half_end(s):
            multiply(1, 0, HOPS, s * near, near)
            wait_flat(15 + s, near)
            multiply(1, 1, HOPS, s * near, near)
            finish(1, s * near, near)

        leave(3, {
            0: lambda: half_own(0), 1: lambda: half_other(0), 2: lambda: half_end(0), 3: lambda: half_own(1)
        })
        half_other(1)
        half_end(1)

    @pl.when(h == 1)
    def _():
        def number_of(b, i, s):
            return i if b == 0 else batch + i + s

        def flat_ref(p, j, way, place):
            if j < HOPS:
                return flat.at[place, pl.ds(p * piece, piece)]
            return flat.at[place, pl.ds(p * piece + way * (piece // 2), piece // 2)]

        def send_flat(p, j, way):
            ref = flat_ref(p, j, way, place_of(j - 1, way))
            remote(
                ref, ref, out_send.at[4 if j < HOPS else 5], ring_recv.at[p, j - 1], toward_way(way)
            ).start()

        def hop(j, between=None):
            for p in range(pieces):
                if p == 2 and between is not None:
                    between()
                span = pl.ds(p * piece, piece)
                ref = flat.at[pl.ds(0, 2), span] if j < HOPS else flat.at[0, span]
                wait_bytes(ref, ring_recv.at[p, j - 1])
                if j < HOPS:
                    for way in range(2):
                        send_flat(p, j + 1, way)

        def send_rows(b, i):
            place = place_at(offset[i])
            for g in range(max(1, b * batch), (b + 1) * batch):
                recv = arrive.at[number_of(b, i, (g - batch) // near if b == 1 and i == RING - 1 else 0)]
                remote(
                    send.at[place, rows_of(g)], x.at[1, place, rows_of(g)], out_send.at[0], recv,
                    (toward(g), lev),
                ).start()

        def arrived(b, i, s=None):
            place = place_at(offset[i])
            start, count = (b * batch, batch) if s is None else (b * batch + s * near, near)
            number = number_of(b, i, s or 0)
            base = max(1, start)
            wait_bytes(
                x.at[1, place, pl.ds(base * cap, (start + count - base) * cap)], arrive.at[number]
            )
            ref = x.at[1, place, pl.ds(start * cap, count * cap)]
            remote(ref, ref, out_send.at[2], twin_recv.at[number], (c, twin)).start()

        for p in range(pieces):
            for way in range(2):
                send_flat(p, 1, way)
        def pass_on(b, *numbers):
            for i in numbers:
                route(place_at(offset[i]), b, 1)
                send_rows(b, i)

        pass_on(0, 0)
        make_pick()
        moved_copy.start()
        hop(1, lambda: pass_on(1, 0))
        pass_on(0, 1, 2)
        send_offsets()
        arrived(0, 0)
        wait_weights()
        multiply(0, 1, 0, fresh=True)
        hop(2)
        pass_on(0, 3, 4)
        pass_on(1, 1)
        arrived(0, 1)
        arrived(0, 2)
        multiply_two(0, 1, 1)
        hop(3)
        pass_on(0, 5, 6)
        pass_on(1, 2)
        wait_padded(0, 1, 0, batch)
        multiply(0, 0, 0)
        hop(HOPS)
        pass_on(0, 7)
        arrived(0, 3)
        arrived(0, 4)
        pass_on(1, 3, 4)
        multiply_two(0, 1, 2)
        pass_on(1, 5, 6)
        wait_padded(1, 2, 0, batch)
        multiply_two(0, 0, 1)
        pass_on(1, 7)
        arrived(0, 5)
        arrived(1, 0)
        multiply(0, 1, -3)
        wait_padded(2, 2, 0, batch)
        multiply_two(0, 0, 2)
        arrived(1, 1)
        arrived(1, 2)
        wait_padded(3, 2, 0, batch)
        multiply_two(0, 0, 3)
        multiply(1, 1, 0, fresh=True)
        arrived(0, 6)
        multiply(0, 1, 3)
        arrived(0, 7)
        multiply(0, 1, HOPS)
        wait_padded(HOPS, 1, 0, batch)
        multiply(0, 0, HOPS)
        finish(0, 0, batch)
        wait_padded(5, 1, batch, batch)
        multiply(1, 0, 0)
        arrived(1, 3)
        arrived(1, 4)
        multiply_two(1, 1, 1)
        wait_padded(6, 2, batch, batch)
        multiply_two(1, 0, 1)
        arrived(1, 5)
        arrived(1, 6)
        multiply_two(1, 1, 2)
        arrived(1, 7, 0)
        wait_padded(7, 2, batch, batch)
        multiply_two(1, 0, 2)
        arrived(1, 7, 1)
        multiply_two(1, 1, 3)
        wait_padded(8, 2, batch, batch)
        multiply_two(1, 0, 3)
        for s in range(2):
            multiply(1, 1, HOPS, s * near, near)
            wait_padded(5 + HOPS + s, 1, batch + s * near, near)
            multiply(1, 0, HOPS, s * near, near)
            finish(1, s * near, near)

    result[...] = collect(0, batch)
    result[...] += collect(batch, near)
    total = result[...] + collect(batch + near, near)
    sources[...] = total.astype(BF16)

    moved_copy.wait()
    rest = pl.ds(cap, (groups - 1) * cap)

    @pl.when(h == 0)
    def _():
        wait_bytes(send.at[0, rest], out_send.at[0])
        wait_bytes(x.at[0, pl.ds(0, 2 * HOPS - 2)], out_send.at[4])
        wait_bytes(x.at[0, 0], out_send.at[5])

    @pl.when(h == 1)
    def _():
        wait_bytes(send.at[:, rest], out_send.at[0])
        wait_bytes(flat.at[pl.ds(0, 2 * HOPS - 2)], out_send.at[4])
        wait_bytes(flat.at[0], out_send.at[5])

    wait_bytes(off_recv.at[pl.ds(1, groups - 1)], out_send.at[1])
    wait_bytes(x.at[0], out_send.at[2])
    wait_bytes(back_send.at[rest], out_send.at[3])


def shards(
    populations, face_speed, cell_class, class_offset, rate_matrix, slope_matrix, rate_scale, slope_scale
):
    rows, width = populations.shape
    groups = SIDE * SIDE
    cap = 2 * rows // groups
    slots = groups * cap
    vmem = pl.BlockSpec(memory_space=pltpu.VMEM)
    hbm = pl.BlockSpec(memory_space=pl.ANY)
    dma = pltpu.SemaphoreType.DMA
    narrow_sources, transported = pl.pallas_call(
        kernel,
        out_shape=(
            jax.ShapeDtypeStruct((rows, width), BF16), jax.ShapeDtypeStruct((rows, width), F32)
        ),
        in_specs=[hbm] * 8,
        out_specs=(vmem, hbm),
        scratch_shapes=[
            pltpu.VMEM((4, rows // 4), I32),
            pltpu.VMEM(class_offset.shape, BF16),
            pltpu.VMEM(face_speed.shape, F32),
            pltpu.VMEM((1, width), F32),
            pltpu.VMEM((1, width), F32),
            pltpu.VMEM((rows + 16, width), F32),
            pltpu.VMEM((2 * RING, width, width), BF16),
            pltpu.VMEM((2 * RING, width, width), BF16),
            pltpu.VMEM((2, RING, slots, width), BF16),
            pltpu.VMEM((RING, rows, width), BF16),
            pltpu.VMEM((RING, slots, width), BF16),
            pltpu.VMEM((groups // 2, 16, 128), BF16),
            pltpu.VMEM((groups, 16, 128), BF16),
            pltpu.VMEM((slots, width), BF16),
            pltpu.VMEM((slots, width), BF16),
            pltpu.VMEM((slots, rows), BF16),
            pltpu.VMEM((rows, slots), BF16),
            pltpu.VMEM((rows, width), F32),
            pltpu.VMEM((2, slots, width), F32),
            pltpu.VMEM((rows, width), F32),
            dma((8,)),
            dma((2,)),
            dma((2,)),
            dma((6,)),
            dma((2 * RING + 1,)),
            dma((groups, HOPS)),
            dma((2 * RING + 1,)),
            dma((3,)),
            dma((3,)),
        ],
        compiler_params=pltpu.CompilerParams(
            collective_id=0, has_side_effects=True, vmem_limit_bytes=60 * 1024 * 1024
        ),
    )(
        cell_class.reshape(4, -1), class_offset, face_speed,
        populations, rate_matrix, slope_matrix, rate_scale, slope_scale,
    )
    sources = narrow_sources.astype(F32)
    return sources, transported + 0.5 * sources


def solution(mesh):
    in_specs = (
        P("cells", "levels"),
        P(),
        P("cells", None),
        P("cells"),
        P("cells", "levels", None),
        P("cells", "levels", None),
        P("cells", "levels"),
        P("cells", "levels"),
    )
    out_specs = (P("cells", "levels"), P("cells", "levels"))
    return jax.shard_map(shards, mesh=mesh, in_specs=in_specs, out_specs=out_specs, check_vma=False)
```
